32 devices in a mesh: dec: 2 (over x), ada: 16 (over z, y, core).
Axes of the slice: x: 2, y: 2, z: 4, core: 2. Of those that a mesh axis runs over, the one named last changes fastest.
Arguments:
- inputs: bfloat16 [4, 64, 8192], P(None, ('dec', 'ada')), may hold values from -6 to 6
- query_weight: bfloat16 [8192, 8192], P(None, 'ada'), may hold values from -0.0625 to 0.0625
- adapter_down: bfloat16 [32, 8192, 64], P(('dec', 'ada')), may hold values from -0.0625 to 0.0625
- adapter_up: bfloat16 [32, 64, 8192], P(('dec', 'ada')), may hold values from -0.75 to 0.75
- adapter_ids: int32 [64, 1], P(('dec', 'ada')), may hold values from 0 to 15; in each aligned block of 32 rows (0 to 31, 32 to 63, ...) at most 4 rows name the same one
- new_cache: bfloat16 [4, 64, 2, 1024], P(None, ('dec', 'ada')), may hold values from -9 to 9
- cache_pool: bfloat16 [256, 2, 16, 1024], P(('dec', 'ada')), may hold values from -400 to 400
- page_table: int32 [64, 4], P(('dec', 'ada')), may hold values from 0 to 15, as said below
- lengths: int32 [64], P(('dec', 'ada')), may hold values from 1 to 64, as said below
Outputs:
- attended: bfloat16 [4, 64, 8192], P(None, ('dec', 'ada'))
The draws below stay inside these ranges and needn't reach their ends.
Inputs may be any that keep to these rules, and one draw needn't show every extreme that they name: `adapter_ids`: in each aligned block of 32 rows (one decode group) no id is named by more than 4 rows, a bound that some block reaches. `page_table`: entries j >= ceil(lengths[r] / 16) are unused. Among rows with the same (r % 32) // 2, the live entries are all different. `lengths`: among rows with the same (r % 32) // 2, one reaches 64.
All inputs are finite; a program needn't handle non-finite values.
Results may differ from the reference program's by a relative error of at most 0.007.
The reference program's roundings to bfloat16 on the way count: a program that leaves them out, or rounds other values in their place, can miss the bound.
Values may be sent and summed in bfloat16 or wider, within the bound.
A program may use at most 64 MiB of HBM per device.

```python
import math
from functools import reduce
import jax
import jax.numpy as jnp
import numpy as np
from jax import lax

D = 8192
HEADS = 64
KVH = 8
HD = 128
RANK = 64
STEPS = 4
PAGE = 16
MAXP = 4
ROW_DEV = 2
CAP = 4
ROWS = 64
GROUP_ROWS = 32
GROUP_ADP = 16
ADAPTERS = 32
POOL_DEV = 8
POOL_GROUP = 128
POOLS = 256
N_DEC = 2
N_ADA = 16


def page_layout(key):
    column_rows = N_DEC * ROW_DEV
    total = N_DEC * POOL_DEV
    key_count, key_forced, key_extra, key_order = jax.random.split(jax.random.fold_in(key, 7), 4)
    counts = jax.random.randint(key_count, (N_ADA, column_rows), 1, MAXP + 1)
    forced = jax.random.randint(key_forced, (N_ADA, 1), 0, column_rows)
    position = jnp.arange(column_rows)[None, :]
    counts = jnp.where(position == forced, MAXP, counts)
    extra = jax.random.randint(key_extra, (N_ADA, column_rows), 0, PAGE)
    lengths = jnp.where(position == forced, MAXP * PAGE, (counts - 1) * PAGE + 1 + extra)
    orders = jax.vmap(lambda subkey: jax.random.permutation(subkey, total))(jax.random.split(key_order, N_ADA))
    starts = jnp.cumsum(counts, axis=1) - counts
    index = (starts[:, :, None] + jnp.arange(MAXP)[None, None, :]) % total
    table = jax.vmap(lambda order, where: order[where])(orders, index)
    table = jnp.transpose(table.reshape(N_ADA, N_DEC, ROW_DEV, MAXP), (1, 0, 2, 3)).reshape(ROWS, MAXP)
    lengths = jnp.transpose(lengths.reshape(N_ADA, N_DEC, ROW_DEV), (1, 0, 2)).reshape(ROWS)
    return (table.astype(jnp.int32), lengths.astype(jnp.int32))


def draw_page_table(key, part):
    return page_layout(key)[0]


def draw_lengths(key, part):
    return page_layout(key)[1]


def draw_cache_pool(key, part):
    width = KVH * HD
    key_keys, key_flag, key_scale, key_vals = jax.random.split(jax.random.fold_in(key, 11), 4)
    halves = jnp.clip(jax.random.normal(key_keys, (POOLS, 1, PAGE // 2, 1, width), jnp.float32), -6.0, 6.0)
    scale = jnp.exp(jax.random.uniform(key_scale, (POOLS, 1, 1, width), jnp.float32, -1.4, 1.4))
    other = jnp.clip(jax.random.normal(key_flag, (POOLS, 1, PAGE // 2, 1, width), jnp.float32), -6.0, 6.0)
    keys = jnp.concatenate([halves, other], axis=3).reshape(POOLS, 1, PAGE, width) * scale
    values = jnp.clip(jax.random.normal(key_vals, (POOLS, 1, PAGE, width), jnp.float32), -6.0, 6.0)
    return jnp.concatenate([keys, values], axis=1).astype(jnp.bfloat16)


def block_levels(own_key, dims, shards, low, high):
    level, own = 1.0, jax.random.fold_in(own_key, 6)
    for axis_at, blocks in shards:
        draws = jnp.exp(jax.random.uniform(jax.random.fold_in(own, axis_at), (blocks,), jnp.float32, low / len(shards), high / len(shards)))
        level = level * jnp.repeat(draws, dims[axis_at] // blocks).reshape([-1 if axis == axis_at else 1 for axis in range(len(dims))])
    return level


def shared_out(rng, own, number, rows, number_of, top, bound, skew):
    order = jax.random.permutation(rng, number_of)
    packed, common = portions_of(number_of, rows * top, bound, skew, True), portions_of(number_of, rows * top, bound, skew, False)
    places = jnp.arange(number_of)

    def named(tallies, turn):
        used = int((tallies > 0).sum())
        fixed = max(1, used // 4)
        moved = fixed + (places - fixed + turn * (used - fixed)) % max(1, number_of - fixed)
        return jnp.zeros((number_of,), jnp.int32).at[order[jnp.where(places < fixed, places, moved)]].set(jnp.asarray(tallies, jnp.int32))

    tallies = jnp.where(number % 4 == 0, named(packed, number // 4), named(common, number - number // 4 - 1))
    mixed = jax.random.permutation(jax.random.fold_in(own, 3), number_of)
    giver, sink = mixed[0:number_of // 2 * 2:2], mixed[1:number_of // 2 * 2:2]
    margin = jnp.minimum(tallies[giver] - 1, bound - tallies[sink]) // 2
    margin = jnp.where((giver == order[0]) | (sink == order[0]) | (tallies[sink] == 0), 0, jnp.maximum(margin, 0))
    moved = jax.random.randint(jax.random.fold_in(own, 4), (number_of // 2,), 0, 1 << 20) % (margin + 1)
    tallies = tallies.at[giver].add(-moved).at[sink].add(moved)
    labels = jnp.searchsorted(jnp.cumsum(tallies), jnp.arange(rows * top), side="right").astype(jnp.int32)
    listing = labels.reshape(top, rows).T
    listing = listing[jax.random.permutation(jax.random.fold_in(own, 1), rows)]
    turn = jax.random.randint(jax.random.fold_in(own, 2), (rows, 1), 0, top)
    return jnp.take_along_axis(listing, (jnp.arange(top)[None, :] + turn) % top, axis=1)


def portions_of(number_of, total, bound, lean, full):
    weights = [(1 << 20) // math.isqrt(grade ** lean) + 1 for grade in range(1, number_of + 1)]
    largest = bound if full else min(bound, max(-(-total // number_of), total * weights[0] // sum(weights)))
    least = 1 if total - largest >= number_of - 1 else 0
    holding, rest = [largest] + [least] * (number_of - 1), total - largest - least * (number_of - 1)
    while rest > 0:
        free = [i for i in range(1, number_of) if holding[i] < largest] or [i for i in range(1, number_of) if holding[i] < bound]
        whole, remaining = sum([weights[i] for i in free]), rest
        for i in free:
            addition = min(bound - holding[i], max(1, remaining * weights[i] // whole), rest)
            holding[i] = holding[i] + addition
            rest = rest - addition
    return np.array(holding)


def gaussian(key, shape, spread, limit, pieces=(), kind=jnp.bfloat16):
    drawn = jax.random.normal(key, shape, jnp.float32) * spread
    if len(pieces) > 0:
        drawn = block_levels(key, shape, pieces, -0.22, 0.18) * drawn
    return jnp.clip(drawn, min=-limit, max=limit).astype(kind)


def setup_inputs(seed: int = 0) -> dict:
    arg_keys = jax.random.split(jax.random.key(seed), 10)
    inputs = gaussian(arg_keys[0], (STEPS, ROWS, D), 1.0, 6.0, ((1, 32),))
    query_weight = gaussian(arg_keys[1], (D, D), D ** -0.5, 0.0625, ((1, 16),))
    adapter_down = gaussian(arg_keys[2], (ADAPTERS, D, RANK), D ** -0.5, 0.0625, ((0, 32),))
    adapter_up = gaussian(arg_keys[3], (ADAPTERS, RANK, D), RANK ** -0.5, 0.75, ((0, 32),))
    adapter_ids_keys = jax.random.split(jax.random.fold_in(arg_keys[4], 1), ROWS // GROUP_ROWS)
    adapter_ids_turns = jax.random.permutation(jax.random.fold_in(arg_keys[4], 3), ROWS // GROUP_ROWS)
    adapter_ids = jax.vmap(lambda own, number: shared_out(jax.random.fold_in(arg_keys[4], 2), own, number, GROUP_ROWS, GROUP_ADP, 1, CAP, 1))(adapter_ids_keys, adapter_ids_turns).reshape((ROWS, 1))
    new_cache = gaussian(arg_keys[5], (STEPS, ROWS, 2, KVH * HD), 1.5, 9.0, ((1, 32),))
    cache_pool = draw_cache_pool(jax.random.fold_in(arg_keys[9], 71), 0)
    page_table = draw_page_table(jax.random.fold_in(arg_keys[9], 71), 0)
    lengths = draw_lengths(jax.random.fold_in(arg_keys[9], 71), 0)
    return {"inputs": inputs, "query_weight": query_weight, "adapter_down": adapter_down, "adapter_up": adapter_up, "adapter_ids": adapter_ids, "new_cache": new_cache, "cache_pool": cache_pool, "page_table": page_table, "lengths": lengths}


NEGATIVE = -1e+30
HIGH = lax.Precision.HIGHEST

def cache_part(query, keys, values, live):
    scale = 1.0 / math.sqrt(query.shape[-1])
    scores = jnp.einsum('trkgd,rpkd->trkgp', query.astype(jnp.float32), keys.astype(jnp.float32), precision=HIGH) * scale
    mask = live[None, :, None, None, :]
    scores = jnp.where(mask, scores, NEGATIVE)
    top = lax.optimization_barrier(jnp.max(scores, axis=-1))
    weights = jnp.where(mask, jnp.exp(scores - top[..., None]), 0.0)
    numerator = jnp.einsum('trkgp,rpkd->trkgd', weights, values.astype(jnp.float32), precision=HIGH)
    return (numerator, top, lax.optimization_barrier(jnp.sum(weights, axis=-1)))

def fresh_part(query, new_entries):
    steps, rows, kv_heads, group, head_dim = query.shape
    scale = 1.0 / math.sqrt(head_dim)
    keys = new_entries[:, :, 0].reshape(new_entries.shape[0], rows, kv_heads, head_dim)
    values = new_entries[:, :, 1].reshape(new_entries.shape[0], rows, kv_heads, head_dim)
    scores = jnp.einsum('trkgd,urkd->trkgu', query.astype(jnp.float32), keys.astype(jnp.float32), precision=HIGH) * scale
    allowed = (jnp.arange(new_entries.shape[0])[None, :] <= jnp.arange(steps)[:, None])[:, None, None, None, :]
    scores = jnp.where(allowed, scores, NEGATIVE)
    top = lax.optimization_barrier(jnp.max(scores, axis=-1))
    weights = jnp.where(allowed, jnp.exp(scores - top[..., None]), 0.0)
    numerator = jnp.einsum('trkgu,urkd->trkgd', weights, values.astype(jnp.float32), precision=HIGH)
    return (numerator, top, lax.optimization_barrier(jnp.sum(weights, axis=-1)))

def finish(parts):
    top = reduce(jnp.maximum, [part[1] for part in parts])
    numerator = sum((part[0] * jnp.exp(part[1] - top)[..., None] for part in parts))
    total = sum((part[2] * jnp.exp(part[1] - top) for part in parts))
    return (numerator / total[..., None]).astype(jnp.bfloat16)

def reference(inputs, query_weight, adapter_down, adapter_up, adapter_ids, new_cache, cache_pool, page_table, lengths):
    base_output = jnp.dot(inputs.reshape(STEPS * ROWS, D), query_weight, preferred_element_type=jnp.float32).reshape(STEPS, ROWS, D)

    def one_block(block):
        first = (block * ROW_DEV).astype(jnp.int32)
        rows = first + jnp.arange(ROW_DEV, dtype=jnp.int32)
        input_block = lax.dynamic_slice_in_dim(inputs, first, ROW_DEV, 1)
        base_block = lax.dynamic_slice_in_dim(base_output, first, ROW_DEV, 1)
        entry = rows // GROUP_ROWS * GROUP_ADP + adapter_ids[rows, 0]
        down = adapter_down[entry]
        upward = adapter_up[entry]
        shrink = jnp.einsum('trd,rdk->trk', input_block.astype(jnp.float32), down.astype(jnp.float32), precision=HIGH).astype(jnp.bfloat16)
        delta = jnp.einsum('trk,rkd->trd', shrink.astype(jnp.float32), upward.astype(jnp.float32), precision=HIGH).astype(jnp.bfloat16)
        query = (base_block + delta.astype(jnp.float32)).astype(jnp.bfloat16)
        query = query.reshape(STEPS, ROW_DEV, KVH, HEADS // KVH, HD)
        table = page_table[rows]
        column = (rows % GROUP_ROWS // ROW_DEV)[:, None]
        slot = table // POOL_DEV * POOL_GROUP + column * POOL_DEV + table % POOL_DEV
        pages = cache_pool[slot]
        keys = pages[:, :, 0].reshape(ROW_DEV, MAXP * PAGE, KVH, HD)
        values = pages[:, :, 1].reshape(ROW_DEV, MAXP * PAGE, KVH, HD)
        live = jnp.arange(MAXP * PAGE, dtype=jnp.int32)[None, :] < lengths[rows][:, None]
        new_block = lax.dynamic_slice_in_dim(new_cache, first, ROW_DEV, 1)
        parts = [cache_part(query, keys, values, live), fresh_part(query, new_block)]
        return finish(parts).reshape(STEPS, ROW_DEV, D)
    outputs = lax.map(one_block, jnp.arange(ROWS // ROW_DEV, dtype=jnp.int32))
    return jnp.transpose(outputs, (1, 0, 2, 3)).reshape(STEPS, ROWS, D)
```

```python
import functools
import math

import jax
import jax.numpy as jnp
from jax import lax
from jax.experimental import pallas as pl
from jax.experimental.pallas import tpu as pltpu
from jax.sharding import PartitionSpec as P

HD = 128
CAP = 4
LANES = 128
GROUPS = 2
PARTS = 1
PIECES = GROUPS * PARTS
STRIDE = 6.0
REACH = 1
BASEEARLY = 0
FARFIRST = 0
AHEAD = 4
NEGATIVE = -1e30
MESH = pl.DeviceIdType.MESH
F32 = jnp.float32
BF16 = jnp.bfloat16


def nt_dot(a, b):
    return lax.dot_general(a, b, (((1,), (1,)), ((), ())), preferred_element_type=F32)


def iota(shape, axis):
    return lax.broadcasted_iota(jnp.int32, shape, axis)


def kernel(
    n,
    n_dec,
    x_hbm,
    w_hbm,
    down_hbm,
    up_hbm,
    ids_hbm,
    new_hbm,
    pool_hbm,
    table_hbm,
    len_hbm,
    out_ref,
    *scratch,
):
    gathered = scratch[:PIECES]
    (
        x_ref, ids_ref, new_ref, table_ref, len_ref, w_ref, down_ref, up_ref, pages, base, shrink,
        d_send, d_recv, q_send, q_recv, keys, values, result,
        early_sem, w_sem, down_sem, up_sem, pool_sem, pool_send, pool_recv,
        far_send, up_send, low_send, across_send, side_send, g_recv, ds_sem, dr_sem, qs_sem, qr_sem,
    ) = scratch[PIECES:]
    early = [
        pltpu.make_async_copy(source, target, early_sem.at[i])
        for i, (source, target) in enumerate(
            [(x_hbm, x_ref), (ids_hbm, ids_ref), (new_hbm, new_ref), (table_hbm, table_ref), (len_hbm, len_ref)]
        )
    ]
    for copy in early:
        copy.start()
    ada, dec = lax.axis_index("ada"), lax.axis_index("dec")
    steps, rows, width = x_ref.shape
    part = width // PARTS
    span_steps = steps // GROUPS
    block = span_steps * rows
    total = n * block
    head_cols = w_ref.shape[1]
    slots = span_steps * CAP
    span = n // 4
    o, m, c = ada // 4, (ada // 2) % 2, ada % 2
    sibling = ada + 1 - 2 * c
    opposite = ada + 2 - 4 * m
    pool_local = pool_hbm.shape[0]

    def w_copy(k):
        where = pl.ds(k * part, part)
        return pltpu.make_async_copy(w_hbm.at[where], w_ref.at[where], w_sem.at[k])

    down_copy = pltpu.make_async_copy(down_hbm, down_ref, down_sem)
    up_copy = pltpu.make_async_copy(up_hbm, up_ref, up_sem)
    own_pages = pages.at[pl.ds(dec * pool_local, pool_local)]
    pool_copy = pltpu.make_async_copy(pool_hbm, own_pages, pool_sem)

    barrier = pltpu.get_barrier_semaphore()

    def greet(peer):
        pl.semaphore_signal(barrier, inc=1, device_id={"ada": peer}, device_id_type=MESH)

    greet(opposite)
    greet(sibling)
    reach = min(REACH, span - 1)
    line_peers = 0
    for distance in range(1, reach + 1):
        for side in (1, -1):

            @pl.when((o + side * distance >= 0) & (o + side * distance < span))
            def _():
                greet(ada + 4 * side * distance)

        line_peers += (o >= distance).astype(jnp.int32) + (o + distance < span).astype(jnp.int32)
    for d in range(1, n_dec):
        pl.semaphore_signal(
            barrier, inc=1, device_id={"dec": lax.rem(dec + d, n_dec)}, device_id_type=MESH
        )
    down_copy.start()
    for k in range(PARTS):
        w_copy(k).start()
    up_copy.start()
    pool_copy.start()

    early[0].wait()
    early[1].wait()
    row_of = iota((block, LANES), 0) % rows
    id_block = jnp.zeros((block, LANES), F32)
    for r in range(rows):
        id_block = jnp.where(row_of == r, ids_ref[r].astype(F32), id_block)
    gathered[0][ada, :, part : part + LANES] = id_block.astype(BF16)
    for g in range(GROUPS):
        mine = jnp.concatenate(
            [x_ref[g * span_steps + t].astype(F32) for t in range(span_steps)], axis=0
        ).astype(BF16)
        for k in range(PARTS):
            gathered[g * PARTS + k][ada, :, 0:part] = mine[:, k * part : (k + 1) * part]
    pl.semaphore_wait(barrier, line_peers + 2 + n_dec - 1)

    def relay(k, source, send_sem, peer):
        return pltpu.make_async_remote_copy(
            src_ref=gathered[k].at[source],
            dst_ref=gathered[k].at[source],
            send_sem=send_sem,
            recv_sem=g_recv.at[k, source],
            device_id={"ada": peer},
            device_id_type=MESH,
        )

    def arrived(k, source):
        relay(k, source, side_send.at[k, 0], sibling).wait_recv()

    def upward(k, line):
        return relay(k, line * 4 + m * 2 + c, up_send.at[k, line], ada + 4)

    def far_up(k, distance):
        return relay(k, ada, far_send.at[k, distance], ada + 4 * distance)

    def far_down(k, distance):
        return relay(k, ada, far_send.at[k, reach + distance], ada - 4 * distance)

    def downward(k, line):
        return relay(k, line * 4 + m * 2 + c, low_send.at[k, line], ada - 4)

    def across(k, line):
        return relay(k, line * 4 + m * 2 + c, across_send.at[k, line], opposite)

    def sideways(k, line, column):
        return relay(
            k, line * 4 + column * 2 + c, side_send.at[k, line * 2 + column], sibling
        )

    def send_line(k, distance):
        @pl.when(o + distance < span)
        def _():
            far_up(k, distance).start()

        @pl.when(o >= distance)
        def _():
            far_down(k, distance).start()

    def send_own(k):
        far = range(1, reach + 1)
        for distance in reversed(far) if FARFIRST else far:
            send_line(k, distance)
        across(k, o).start()
        sideways(k, o, m).start()

    def line_event(k, distance):
        below, above = o - distance, o + distance

        @pl.when(below >= 0)
        def _():
            arrived(k, below * 4 + m * 2 + c)

            if distance >= reach:

                @pl.when(o < span - 1)
                def _():
                    upward(k, below).start()

            across(k, below).start()
            sideways(k, below, m).start()

        @pl.when(above < span)
        def _():
            arrived(k, above * 4 + m * 2 + c)

            if distance >= reach:

                @pl.when(o > 0)
                def _():
                    downward(k, above).start()

            across(k, above).start()
            sideways(k, above, m).start()

    def across_event(k, distance):
        other = 1 - m
        below, above = o - distance, o + distance

        @pl.when(below >= 0)
        def _():
            arrived(k, below * 4 + other * 2 + c)
            sideways(k, below, other).start()

        if distance:

            @pl.when(above < span)
            def _():
                arrived(k, above * 4 + other * 2 + c)
                sideways(k, above, other).start()

    def side_wave(k):
        for line in range(span):
            for column in range(2):
                arrived(k, line * 4 + column * 2 + 1 - c)

    def piece_rows(g, k):
        held = gathered[g * PARTS + k]
        return jnp.concatenate(
            [held[source, :, 0:part].astype(F32) for source in range(n)], axis=0
        ).astype(BF16)

    def add_shrink(g):
        for k in range(PARTS):
            term = nt_dot(piece_rows(g, k), down_ref[:, k * part : (k + 1) * part])
            shrink[g] = term if k == 0 else shrink[g] + term

    def add_base(g):
        for k in range(PARTS):
            term = jnp.dot(
                piece_rows(g, k),
                w_ref[k * part : (k + 1) * part, :],
                preferred_element_type=F32,
            )
            base[g] = term if k == 0 else base[g] + term

    def pool_send_copy(d):
        return pltpu.make_async_remote_copy(
            src_ref=pool_hbm,
            dst_ref=own_pages,
            send_sem=pool_send.at[d],
            recv_sem=pool_recv.at[dec],
            device_id={"dec": lax.rem(dec + d, n_dec)},
            device_id_type=MESH,
        )

    def pool_arrived(owner):
        pltpu.make_async_remote_copy(
            src_ref=pool_hbm,
            dst_ref=pages.at[pl.ds(owner * pool_local, pool_local)],
            send_sem=pool_send.at[1],
            recv_sem=pool_recv.at[owner],
            device_id={"dec": lax.rem(dec + 1, n_dec)},
            device_id_type=MESH,
        ).wait_recv()

    def slot_masks():
        id_col = jnp.concatenate(
            [gathered[0][source, :, part : part + LANES].astype(F32) for source in range(n)], axis=0
        )[:, 0:1]
        at_row, at_lane = iota((total, total), 0), iota((total, total), 1)
        id_row = jnp.sum(jnp.where(at_row == at_lane, id_col, 0.0), axis=0, keepdims=True)
        same = id_col == id_row
        row_rank = at_row // block * rows + at_row % rows
        lane_rank = at_lane // block * rows + at_lane % rows
        count_col = jnp.sum(
            jnp.where(same & (lane_rank < row_rank) & (at_lane % block < rows), 1.0, 0.0),
            axis=1,
            keepdims=True,
        )
        count_row = jnp.sum(
            jnp.where(same & (row_rank < lane_rank) & (at_row % block < rows), 1.0, 0.0),
            axis=0,
            keepdims=True,
        )
        slot, lane = iota((slots, total), 0), iota((slots, total), 1)
        pick = jnp.where(
            (slot // CAP == lane % block // rows)
            & (id_row == ada.astype(F32))
            & (count_row == (slot % CAP).astype(F32)),
            1.0,
            0.0,
        ).astype(BF16)
        row, place = iota((total, n * slots), 0), iota((total, n * slots), 1)
        spread = jnp.where(
            (row % block // rows == place % slots // CAP)
            & (id_col == (place // slots).astype(F32))
            & (count_col == (place % CAP).astype(F32)),
            1.0,
            0.0,
        ).astype(BF16)
        return pick, spread

    entries, page = table_ref.shape[1], pages.shape[2]
    cached = rows * entries * page
    fresh_rows = steps * rows
    kv_heads = keys.shape[1] // HD
    heads = width // HD
    group = heads // kv_heads
    count = keys.shape[0]

    def key_mask(g):
        query_at, key_at = iota((heads * block, count), 0), iota((heads * block, count), 1)
        query_step, query_row = query_at % block // rows + g * span_steps, query_at % rows
        limit = jnp.zeros((heads * block, count), jnp.int32)
        for r in range(rows):
            limit = jnp.where(query_row == r, len_ref[r], limit)
        in_cache = (
            (key_at < cached)
            & (key_at // (entries * page) == query_row)
            & (key_at % (entries * page) < limit)
        )
        late = key_at - cached
        in_new = (late >= 0) & (late % rows == query_row) & (late // rows <= query_step)
        return in_cache | in_new

    def delta_of(g, chosen, target):
        columns = pl.ds(pl.multiple_of(target * head_cols, head_cols), head_cols)
        return jnp.dot(chosen, up_ref[:, columns], preferred_element_type=F32).astype(BF16)

    def d_copy(g, source, target):
        return pltpu.make_async_remote_copy(
            src_ref=d_send.at[g, target],
            dst_ref=d_recv.at[g, source],
            send_sem=ds_sem.at[g, target],
            recv_sem=dr_sem.at[g, source],
            device_id={"ada": target},
            device_id_type=MESH,
        )

    def q_copy(g, source, target):
        return pltpu.make_async_remote_copy(
            src_ref=q_send.at[g, target],
            dst_ref=q_recv.at[g, source],
            send_sem=qs_sem.at[g, target],
            recv_sem=qr_sem.at[g, source],
            device_id={"ada": target},
            device_id_type=MESH,
        )

    order = sorted(range(1, n), key=lambda d: (abs(d - n // 2), d))
    targets = [lax.rem(ada + d, n) for d in order]
    sources = [lax.rem(ada + n - d, n) for d in order]

    def send_delta(g):
        chosen = jnp.dot(pick, shrink[g].astype(BF16), preferred_element_type=F32).astype(BF16)
        for i, target in enumerate(targets):
            d_send[g, target] = delta_of(g, chosen, target)
            if i > 0:
                d_copy(g, ada, targets[i - 1]).start()
        d_recv[g, ada] = delta_of(g, chosen, ada)
        d_copy(g, ada, targets[-1]).start()

    def send_query(g):
        for source in sources:
            d_copy(g, source, source).wait_recv()
        received = d_recv[g].astype(F32).reshape(n * slots, head_cols).astype(BF16)
        update = jnp.dot(spread, received, preferred_element_type=F32)
        query = base[g] + update
        for source in range(n):
            q_send[g, source] = query[source * block : (source + 1) * block].astype(BF16)
        for target in targets:
            q_copy(g, ada, target).start()
        q_recv[g, ada] = q_send[g, ada]

    scale = 1.0 / math.sqrt(HD)
    per_source = head_cols // HD

    def attend(g, allowed):
        for source in sources:
            q_copy(g, source, source).wait_recv()
        scores = []
        for h in range(kv_heads):
            parts = []
            for j in range(group):
                head = h * group + j
                first = head % per_source * HD
                parts.append(q_recv[g, head // per_source, :, first : first + HD].astype(F32))
            query = jnp.concatenate(parts, axis=0).astype(BF16)
            scores.append(nt_dot(query, keys[:, h * HD : (h + 1) * HD]))
        scores = jnp.where(allowed, jnp.concatenate(scores, axis=0) * scale, NEGATIVE)
        top = jnp.max(scores, axis=1, keepdims=True)
        weights = jnp.where(allowed, jnp.exp(scores - top), 0.0)
        denominator = jnp.sum(weights, axis=1, keepdims=True)
        high = weights.astype(BF16)
        low = (weights - high.astype(F32)).astype(BF16)
        height = group * block
        for h in range(kv_heads):
            at, lanes = slice(h * height, (h + 1) * height), slice(h * HD, (h + 1) * HD)
            both = jnp.dot(
                jnp.concatenate([high[at], low[at]], axis=0),
                values[:, lanes],
                preferred_element_type=F32,
            )
            attended = (both[:height] + both[height:]) / denominator[at]
            for j in range(group):
                first = (h * group + j) * HD
                result[g, :, first : first + HD] = attended[j * block : (j + 1) * block]
        for t in range(span_steps):
            out_ref[g * span_steps + t] = result[g, t * rows : (t + 1) * rows, :].astype(BF16)

    events = []
    for p in range(PIECES):
        events.append((p * 1.0 if p < AHEAD else p + STRIDE / 2, 0, p, 0))
        for distance in range(1, span):
            events.append((p + STRIDE * distance, 1, p, distance))
        for distance in range(span):
            events.append((p + STRIDE * (distance + 1), 2, p, distance))
        events.append((p + STRIDE * (span + 1), 3, p, 0))
    events.sort()
    pick = spread = None
    for _, kind, p, distance in events:
        if kind == 0:
            send_own(p)
            if p == min(1, PIECES - 1):
                for d in range(1, n_dec):
                    pool_send_copy(d).start()
        elif kind == 1:
            line_event(p, distance)
        elif kind == 2:
            across_event(p, distance)
        else:
            side_wave(p)
            if p == 0:
                pick, spread = slot_masks()
                down_copy.wait()
                up_copy.wait()
            if p % PARTS == PARTS - 1:
                g = p // PARTS
                add_shrink(g)
                send_delta(g)
                if g == 0:
                    for k in range(PARTS):
                        w_copy(k).wait()
                if BASEEARLY or g == GROUPS - 1:
                    for i in range(g if BASEEARLY else 0, g + 1):
                        add_base(i)

    for copy in early[2:]:
        copy.wait()
    masks = [key_mask(g) for g in range(GROUPS)]
    pool_copy.wait()
    for d in range(1, n_dec):
        pool_arrived(lax.rem(dec + d, n_dec))
    for r in range(rows):
        for j in range(entries):
            held = pages[table_ref[r, j]]
            first = (r * entries + j) * page
            keys[first : first + page, :] = held[0]
            values[first : first + page, :] = held[1]
    fresh = [new_ref[u, r].astype(F32) for u in range(steps) for r in range(rows)]
    empty = jnp.zeros((keys.shape[0] - cached - fresh_rows, keys.shape[1]), F32)
    keys[cached:, :] = jnp.concatenate([f[0:1] for f in fresh] + [empty], axis=0).astype(BF16)
    values[cached:, :] = jnp.concatenate([f[1:2] for f in fresh] + [empty], axis=0).astype(BF16)

    for g in range(GROUPS):
        send_query(g)
    for g in range(GROUPS):
        attend(g, masks[g])

    for k in range(PIECES):
        for distance in range(1, reach + 1):

            @pl.when(o + distance < span)
            def _():
                far_up(k, distance).wait_send()

            @pl.when(o >= distance)
            def _():
                far_down(k, distance).wait_send()

        for line in range(span):
            across(k, line).wait_send()

            @pl.when((line <= o - reach) & (o < span - 1))
            def _():
                upward(k, line).wait_send()

            @pl.when((line >= o + reach) & (o > 0))
            def _():
                downward(k, line).wait_send()

            for column in range(2):
                sideways(k, line, column).wait_send()
    for d in range(1, n_dec):
        pool_send_copy(d).wait_send()
    for g in range(GROUPS):
        for target in targets:
            d_copy(g, ada, target).wait_send()
            q_copy(g, ada, target).wait_send()


def body(
    inputs,
    query_weight,
    adapter_down,
    adapter_up,
    adapter_ids,
    new_cache,
    cache_pool,
    page_table,
    lengths,
):
    n, n_dec = lax.axis_size("ada"), lax.axis_size("dec")
    steps, rows, width = inputs.shape
    held, _, rank = adapter_down.shape
    assert held == 1 and n % 4 == 0
    head_cols = query_weight.shape[1]
    block, slots, span = steps // GROUPS * rows, steps // GROUPS * CAP, n // 4
    part = width // PARTS
    pool_local, _, page, kv_width = cache_pool.shape
    count = -(-(rows * page_table.shape[1] * page + steps * rows) // 16) * 16
    dma = pltpu.SemaphoreType.DMA
    vmem, hbm = pl.BlockSpec(memory_space=pltpu.VMEM), pl.BlockSpec(memory_space=pl.ANY)
    scratch = [
        pltpu.VMEM((n, block, part + (LANES if k == 0 else 0)), BF16) for k in range(PIECES)
    ] + [
        pltpu.VMEM(inputs.shape, BF16),
        pltpu.SMEM((rows,), jnp.int32),
        pltpu.VMEM(new_cache.shape, BF16),
        pltpu.SMEM(page_table.shape, jnp.int32),
        pltpu.SMEM(lengths.shape, jnp.int32),
        pltpu.VMEM((width, head_cols), BF16),
        pltpu.VMEM((rank, width), BF16),
        pltpu.VMEM((rank, width), BF16),
        pltpu.VMEM((n_dec * pool_local, 2, page, kv_width), BF16),
        pltpu.VMEM((GROUPS, n * block, head_cols), F32),
        pltpu.VMEM((GROUPS, n * block, rank), F32),
        pltpu.VMEM((GROUPS, n, slots, head_cols), BF16),
        pltpu.VMEM((GROUPS, n, slots, head_cols), BF16),
        pltpu.VMEM((GROUPS, n, block, head_cols), BF16),
        pltpu.VMEM((GROUPS, n, block, head_cols), BF16),
        pltpu.VMEM((count, kv_width), BF16),
        pltpu.VMEM((count, kv_width), BF16),
        pltpu.VMEM((GROUPS, block, width), F32),
        dma((5,)),
        dma((PARTS,)),
        dma,
        dma,
        dma,
        dma((n_dec,)),
        dma((n_dec,)),
        dma((PIECES, 2 * span)),
        dma((PIECES, span)),
        dma((PIECES, span)),
        dma((PIECES, span)),
        dma((PIECES, 2 * span)),
        dma((PIECES, n)),
        dma((GROUPS, n)),
        dma((GROUPS, n)),
        dma((GROUPS, n)),
        dma((GROUPS, n)),
    ]
    return pl.pallas_call(
        functools.partial(kernel, n, n_dec),
        out_shape=pltpu.VMEM((steps, rows, width), BF16),
        in_specs=[hbm] * 9,
        out_specs=vmem,
        scratch_shapes=scratch,
        compiler_params=pltpu.CompilerParams(
            collective_id=0, has_side_effects=True, vmem_limit_bytes=60 * 1024 * 1024
        ),
    )(
        inputs,
        query_weight,
        jnp.swapaxes(adapter_down[0], 0, 1),
        adapter_up[0],
        adapter_ids[:, 0],
        new_cache,
        cache_pool,
        page_table,
        lengths,
    )


def solution(mesh):
    in_specs = (
        P(None, ("dec", "ada"), None),
        P(None, "ada"),
        P(("dec", "ada"), None, None),
        P(("dec", "ada"), None, None),
        P(("dec", "ada"), None),
        P(None, ("dec", "ada"), None, None),
        P(("dec", "ada"), None, None, None),
        P(("dec", "ada"), None),
        P(("dec", "ada")),
    )
    out_specs = P(None, ("dec", "ada"), None)
    return jax.shard_map(body, mesh=mesh, in_specs=in_specs, out_specs=out_specs, check_vma=False)
```

```python
import functools
import math

import jax
import jax.numpy as jnp
from jax import lax
from jax.experimental import pallas as pl
from jax.experimental.pallas import tpu as pltpu
from jax.sharding import PartitionSpec as P

HD = 128
CAP = 4
LANES = 128
GROUPS = 1
PARTS = 2
PIECES = GROUPS * PARTS
STRIDE = 6.0
NEGATIVE = -1e30
MESH = pl.DeviceIdType.MESH
F32 = jnp.float32
BF16 = jnp.bfloat16


def nt_dot(a, b):
    return lax.dot_general(a, b, (((1,), (1,)), ((), ())), preferred_element_type=F32)


def iota(shape, axis):
    return lax.broadcasted_iota(jnp.int32, shape, axis)


def kernel(
    n,
    n_dec,
    x_hbm,
    w_hbm,
    down_hbm,
    up_hbm,
    ids_hbm,
    new_hbm,
    pool_hbm,
    table_hbm,
    len_hbm,
    out_ref,
    *scratch,
):
    gathered = scratch[:PIECES]
    (
        x_ref, ids_ref, new_ref, table_ref, len_ref, w_ref, down_ref, up_ref, pages, base, shrink,
        d_send, d_recv, q_send, q_recv, keys, values, result,
        early_sem, w_sem, down_sem, up_sem, pool_sem, pool_send, pool_recv,
        up_send, low_send, across_send, side_send, g_recv, ds_sem, dr_sem, qs_sem, qr_sem,
    ) = scratch[PIECES:]
    early = [
        pltpu.make_async_copy(source, target, early_sem.at[i])
        for i, (source, target) in enumerate(
            [(x_hbm, x_ref), (ids_hbm, ids_ref), (new_hbm, new_ref), (table_hbm, table_ref), (len_hbm, len_ref)]
        )
    ]
    for copy in early:
        copy.start()
    ada, dec = lax.axis_index("ada"), lax.axis_index("dec")
    steps, rows, width = x_ref.shape
    part = width // PARTS
    span_steps = steps // GROUPS
    block = span_steps * rows
    total = n * block
    head_cols = w_ref.shape[1]
    slots = span_steps * CAP
    span = n // 4
    o, m, c = ada // 4, (ada // 2) % 2, ada % 2
    sibling = ada + 1 - 2 * c
    opposite = ada + 2 - 4 * m
    pool_local = pool_hbm.shape[0]

    def w_copy(k):
        where = pl.ds(k * part, part)
        return pltpu.make_async_copy(w_hbm.at[where], w_ref.at[where], w_sem.at[k])

    down_copy = pltpu.make_async_copy(down_hbm, down_ref, down_sem)
    up_copy = pltpu.make_async_copy(up_hbm, up_ref, up_sem)
    own_pages = pages.at[pl.ds(dec * pool_local, pool_local)]
    pool_copy = pltpu.make_async_copy(pool_hbm, own_pages, pool_sem)

    barrier = pltpu.get_barrier_semaphore()

    def greet(peer):
        pl.semaphore_signal(barrier, inc=1, device_id={"ada": peer}, device_id_type=MESH)

    greet(opposite)
    greet(sibling)
    for side in (1, -1):

        @pl.when((o + side >= 0) & (o + side < span))
        def _():
            greet(ada + 4 * side)

    line_peers = (o >= 1).astype(jnp.int32) + (o + 1 < span).astype(jnp.int32)
    for d in range(1, n_dec):
        pl.semaphore_signal(
            barrier, inc=1, device_id={"dec": lax.rem(dec + d, n_dec)}, device_id_type=MESH
        )
    down_copy.start()
    for k in range(PARTS):
        w_copy(k).start()
    up_copy.start()
    pool_copy.start()

    early[0].wait()
    early[1].wait()
    row_of = iota((block, LANES), 0) % rows
    id_block = jnp.zeros((block, LANES), F32)
    for r in range(rows):
        id_block = jnp.where(row_of == r, ids_ref[r].astype(F32), id_block)
    gathered[0][ada, :, part : part + LANES] = id_block.astype(BF16)
    for g in range(GROUPS):
        mine = jnp.concatenate(
            [x_ref[g * span_steps + t].astype(F32) for t in range(span_steps)], axis=0
        ).astype(BF16)
        for k in range(PARTS):
            gathered[g * PARTS + k][ada, :, 0:part] = mine[:, k * part : (k + 1) * part]
    pl.semaphore_wait(barrier, line_peers + 2 + n_dec - 1)

    def relay(k, source, send_sem, peer):
        return pltpu.make_async_remote_copy(
            src_ref=gathered[k].at[source],
            dst_ref=gathered[k].at[source],
            send_sem=send_sem,
            recv_sem=g_recv.at[k, source],
            device_id={"ada": peer},
            device_id_type=MESH,
        )

    def arrived(k, source):
        relay(k, source, side_send.at[k, 0], sibling).wait_recv()

    def upward(k, line):
        return relay(k, line * 4 + m * 2 + c, up_send.at[k, line], ada + 4)

    def downward(k, line):
        return relay(k, line * 4 + m * 2 + c, low_send.at[k, line], ada - 4)

    def across(k, line):
        return relay(k, line * 4 + m * 2 + c, across_send.at[k, line], opposite)

    def sideways(k, line, column):
        return relay(
            k, line * 4 + column * 2 + c, side_send.at[k, line * 2 + column], sibling
        )

    def send_own(k):
        @pl.when(o < span - 1)
        def _():
            upward(k, o).start()

        @pl.when(o > 0)
        def _():
            downward(k, o).start()

        across(k, o).start()
        sideways(k, o, m).start()

    def line_event(k, distance):
        below, above = o - distance, o + distance

        @pl.when(below >= 0)
        def _():
            arrived(k, below * 4 + m * 2 + c)

            @pl.when(o < span - 1)
            def _():
                upward(k, below).start()

            across(k, below).start()
            sideways(k, below, m).start()

        @pl.when(above < span)
        def _():
            arrived(k, above * 4 + m * 2 + c)

            @pl.when(o > 0)
            def _():
                downward(k, above).start()

            across(k, above).start()
            sideways(k, above, m).start()

    def across_event(k, distance):
        other = 1 - m
        below, above = o - distance, o + distance

        @pl.when(below >= 0)
        def _():
            arrived(k, below * 4 + other * 2 + c)
            sideways(k, below, other).start()

        if distance:

            @pl.when(above < span)
            def _():
                arrived(k, above * 4 + other * 2 + c)
                sideways(k, above, other).start()

    def side_wave(k):
        for line in range(span):
            for column in range(2):
                arrived(k, line * 4 + column * 2 + 1 - c)

    def piece_rows(g, k):
        held = gathered[g * PARTS + k]
        return jnp.concatenate(
            [held[source, :, 0:part].astype(F32) for source in range(n)], axis=0
        ).astype(BF16)

    def add_shrink(g):
        for k in range(PARTS):
            term = nt_dot(piece_rows(g, k), down_ref[:, k * part : (k + 1) * part])
            shrink[g] = term if k == 0 else shrink[g] + term

    def add_base(g):
        for k in range(PARTS):
            term = jnp.dot(
                piece_rows(g, k),
                w_ref[k * part : (k + 1) * part, :],
                preferred_element_type=F32,
            )
            base[g] = term if k == 0 else base[g] + term

    def pool_send_copy(d):
        return pltpu.make_async_remote_copy(
            src_ref=pool_hbm,
            dst_ref=own_pages,
            send_sem=pool_send.at[d],
            recv_sem=pool_recv.at[dec],
            device_id={"dec": lax.rem(dec + d, n_dec)},
            device_id_type=MESH,
        )

    def pool_arrived(owner):
        pltpu.make_async_remote_copy(
            src_ref=pool_hbm,
            dst_ref=pages.at[pl.ds(owner * pool_local, pool_local)],
            send_sem=pool_send.at[1],
            recv_sem=pool_recv.at[owner],
            device_id={"dec": lax.rem(dec + 1, n_dec)},
            device_id_type=MESH,
        ).wait_recv()

    def slot_masks():
        id_col = jnp.concatenate(
            [gathered[0][source, :, part : part + LANES].astype(F32) for source in range(n)], axis=0
        )[:, 0:1]
        at_row, at_lane = iota((total, total), 0), iota((total, total), 1)
        id_row = jnp.sum(jnp.where(at_row == at_lane, id_col, 0.0), axis=0, keepdims=True)
        same = id_col == id_row
        row_rank = at_row // block * rows + at_row % rows
        lane_rank = at_lane // block * rows + at_lane % rows
        count_col = jnp.sum(
            jnp.where(same & (lane_rank < row_rank) & (at_lane % block < rows), 1.0, 0.0),
            axis=1,
            keepdims=True,
        )
        count_row = jnp.sum(
            jnp.where(same & (row_rank < lane_rank) & (at_row % block < rows), 1.0, 0.0),
            axis=0,
            keepdims=True,
        )
        slot, lane = iota((slots, total), 0), iota((slots, total), 1)
        pick = jnp.where(
            (slot // CAP == lane % block // rows)
            & (id_row == ada.astype(F32))
            & (count_row == (slot % CAP).astype(F32)),
            1.0,
            0.0,
        ).astype(BF16)
        row, place = iota((total, n * slots), 0), iota((total, n * slots), 1)
        spread = jnp.where(
            (row % block // rows == place % slots // CAP)
            & (id_col == (place // slots).astype(F32))
            & (count_col == (place % CAP).astype(F32)),
            1.0,
            0.0,
        ).astype(BF16)
        return pick, spread

    entries, page = table_ref.shape[1], pages.shape[2]
    cached = rows * entries * page
    fresh_rows = steps * rows
    kv_heads = keys.shape[1] // HD
    heads = width // HD
    group = heads // kv_heads
    count = keys.shape[0]

    def key_mask(g):
        query_at, key_at = iota((heads * block, count), 0), iota((heads * block, count), 1)
        query_step, query_row = query_at % block // rows + g * span_steps, query_at % rows
        limit = jnp.zeros((heads * block, count), jnp.int32)
        for r in range(rows):
            limit = jnp.where(query_row == r, len_ref[r], limit)
        in_cache = (
            (key_at < cached)
            & (key_at // (entries * page) == query_row)
            & (key_at % (entries * page) < limit)
        )
        late = key_at - cached
        in_new = (late >= 0) & (late % rows == query_row) & (late // rows <= query_step)
        return in_cache | in_new

    def delta_of(g, chosen, target):
        columns = pl.ds(pl.multiple_of(target * head_cols, head_cols), head_cols)
        return jnp.dot(chosen, up_ref[:, columns], preferred_element_type=F32).astype(BF16)

    def d_copy(g, source, target):
        return pltpu.make_async_remote_copy(
            src_ref=d_send.at[g, target],
            dst_ref=d_recv.at[g, source],
            send_sem=ds_sem.at[g, target],
            recv_sem=dr_sem.at[g, source],
            device_id={"ada": target},
            device_id_type=MESH,
        )

    def q_copy(g, source, target):
        return pltpu.make_async_remote_copy(
            src_ref=q_send.at[g, target],
            dst_ref=q_recv.at[g, source],
            send_sem=qs_sem.at[g, target],
            recv_sem=qr_sem.at[g, source],
            device_id={"ada": target},
            device_id_type=MESH,
        )

    order = range(1, n)
    targets = [lax.rem(ada + d, n) for d in order]
    sources = [lax.rem(ada + n - d, n) for d in order]

    def send_delta(g):
        chosen = jnp.dot(pick, shrink[g].astype(BF16), preferred_element_type=F32).astype(BF16)
        for i, target in enumerate(targets):
            d_send[g, target] = delta_of(g, chosen, target)
            if i > 0:
                d_copy(g, ada, targets[i - 1]).start()
        d_recv[g, ada] = delta_of(g, chosen, ada)
        d_copy(g, ada, targets[-1]).start()

    def send_query(g):
        for source in sources:
            d_copy(g, source, source).wait_recv()
        received = d_recv[g].astype(F32).reshape(n * slots, head_cols).astype(BF16)
        update = jnp.dot(spread, received, preferred_element_type=F32)
        query = base[g] + update
        for source in range(n):
            q_send[g, source] = query[source * block : (source + 1) * block].astype(BF16)
        for target in targets:
            q_copy(g, ada, target).start()
        q_recv[g, ada] = q_send[g, ada]

    scale = 1.0 / math.sqrt(HD)
    per_source = head_cols // HD

    def attend(g, allowed):
        for source in sources:
            q_copy(g, source, source).wait_recv()
        scores = []
        for h in range(kv_heads):
            parts = []
            for j in range(group):
                head = h * group + j
                first = head % per_source * HD
                parts.append(q_recv[g, head // per_source, :, first : first + HD].astype(F32))
            query = jnp.concatenate(parts, axis=0).astype(BF16)
            scores.append(nt_dot(query, keys[:, h * HD : (h + 1) * HD]))
        scores = jnp.where(allowed, jnp.concatenate(scores, axis=0) * scale, NEGATIVE)
        top = jnp.max(scores, axis=1, keepdims=True)
        weights = jnp.where(allowed, jnp.exp(scores - top), 0.0)
        denominator = jnp.sum(weights, axis=1, keepdims=True)
        high = weights.astype(BF16)
        low = (weights - high.astype(F32)).astype(BF16)
        height = group * block
        for h in range(kv_heads):
            at, lanes = slice(h * height, (h + 1) * height), slice(h * HD, (h + 1) * HD)
            both = jnp.dot(
                jnp.concatenate([high[at], low[at]], axis=0),
                values[:, lanes],
                preferred_element_type=F32,
            )
            attended = (both[:height] + both[height:]) / denominator[at]
            for j in range(group):
                first = (h * group + j) * HD
                result[g, :, first : first + HD] = attended[j * block : (j + 1) * block]
        for t in range(span_steps):
            out_ref[g * span_steps + t] = result[g, t * rows : (t + 1) * rows, :].astype(BF16)

    events = []
    for p in range(PIECES):
        events.append((p * 1.0, 0, p, 0))
        for distance in range(1, span):
            events.append((p + STRIDE * distance, 1, p, distance))
        for distance in range(span):
            events.append((p + STRIDE * (distance + 1), 2, p, distance))
        events.append((p + STRIDE * (span + 1), 3, p, 0))
    events.sort()
    pick = spread = None
    for _, kind, p, distance in events:
        if kind == 0:
            send_own(p)
            if p == min(1, PIECES - 1):
                for d in range(1, n_dec):
                    pool_send_copy(d).start()
        elif kind == 1:
            line_event(p, distance)
        elif kind == 2:
            across_event(p, distance)
        else:
            side_wave(p)
            if p == 0:
                pick, spread = slot_masks()
                down_copy.wait()
                up_copy.wait()
            if p % PARTS == PARTS - 1:
                g = p // PARTS
                add_shrink(g)
                send_delta(g)
                if g == 0:
                    for k in range(PARTS):
                        w_copy(k).wait()
                if g == GROUPS - 1:
                    for i in range(g + 1):
                        add_base(i)

    for copy in early[2:]:
        copy.wait()
    masks = [key_mask(g) for g in range(GROUPS)]
    pool_copy.wait()
    for d in range(1, n_dec):
        pool_arrived(lax.rem(dec + d, n_dec))
    for r in range(rows):
        for j in range(entries):
            held = pages[table_ref[r, j]]
            first = (r * entries + j) * page
            keys[first : first + page, :] = held[0]
            values[first : first + page, :] = held[1]
    fresh = [new_ref[u, r].astype(F32) for u in range(steps) for r in range(rows)]
    empty = jnp.zeros((keys.shape[0] - cached - fresh_rows, keys.shape[1]), F32)
    keys[cached:, :] = jnp.concatenate([f[0:1] for f in fresh] + [empty], axis=0).astype(BF16)
    values[cached:, :] = jnp.concatenate([f[1:2] for f in fresh] + [empty], axis=0).astype(BF16)

    for k in range(PIECES):
        for line in range(span):
            across(k, line).wait_send()

            @pl.when((line <= o) & (o < span - 1))
            def _():
                upward(k, line).wait_send()

            @pl.when((line >= o) & (o > 0))
            def _():
                downward(k, line).wait_send()

            for column in range(2):
                sideways(k, line, column).wait_send()
    for d in range(1, n_dec):
        pool_send_copy(d).wait_send()
    for g in range(GROUPS):
        send_query(g)
    for g in range(GROUPS):
        for target in targets:
            d_copy(g, ada, target).wait_send()
    for g in range(GROUPS):
        attend(g, masks[g])

    for g in range(GROUPS):
        for target in targets:
            q_copy(g, ada, target).wait_send()


def body(
    inputs,
    query_weight,
    adapter_down,
    adapter_up,
    adapter_ids,
    new_cache,
    cache_pool,
    page_table,
    lengths,
):
    n, n_dec = lax.axis_size("ada"), lax.axis_size("dec")
    steps, rows, width = inputs.shape
    held, _, rank = adapter_down.shape
    assert held == 1 and n % 4 == 0
    head_cols = query_weight.shape[1]
    block, slots, span = steps // GROUPS * rows, steps // GROUPS * CAP, n // 4
    part = width // PARTS
    pool_local, _, page, kv_width = cache_pool.shape
    count = -(-(rows * page_table.shape[1] * page + steps * rows) // 16) * 16
    dma = pltpu.SemaphoreType.DMA
    vmem, hbm = pl.BlockSpec(memory_space=pltpu.VMEM), pl.BlockSpec(memory_space=pl.ANY)
    scratch = [
        pltpu.VMEM((n, block, part + (LANES if k == 0 else 0)), BF16) for k in range(PIECES)
    ] + [
        pltpu.VMEM(inputs.shape, BF16),
        pltpu.SMEM((rows,), jnp.int32),
        pltpu.VMEM(new_cache.shape, BF16),
        pltpu.SMEM(page_table.shape, jnp.int32),
        pltpu.SMEM(lengths.shape, jnp.int32),
        pltpu.VMEM((width, head_cols), BF16),
        pltpu.VMEM((rank, width), BF16),
        pltpu.VMEM((rank, width), BF16),
        pltpu.VMEM((n_dec * pool_local, 2, page, kv_width), BF16),
        pltpu.VMEM((GROUPS, n * block, head_cols), F32),
        pltpu.VMEM((GROUPS, n * block, rank), F32),
        pltpu.VMEM((GROUPS, n, slots, head_cols), BF16),
        pltpu.VMEM((GROUPS, n, slots, head_cols), BF16),
        pltpu.VMEM((GROUPS, n, block, head_cols), BF16),
        pltpu.VMEM((GROUPS, n, block, head_cols), BF16),
        pltpu.VMEM((count, kv_width), BF16),
        pltpu.VMEM((count, kv_width), BF16),
        pltpu.VMEM((GROUPS, block, width), F32),
        dma((5,)),
        dma((PARTS,)),
        dma,
        dma,
        dma,
        dma((n_dec,)),
        dma((n_dec,)),
        dma((PIECES, span)),
        dma((PIECES, span)),
        dma((PIECES, span)),
        dma((PIECES, 2 * span)),
        dma((PIECES, n)),
        dma((GROUPS, n)),
        dma((GROUPS, n)),
        dma((GROUPS, n)),
        dma((GROUPS, n)),
    ]
    return pl.pallas_call(
        functools.partial(kernel, n, n_dec),
        out_shape=pltpu.VMEM((steps, rows, width), BF16),
        in_specs=[hbm] * 9,
        out_specs=vmem,
        scratch_shapes=scratch,
        compiler_params=pltpu.CompilerParams(
            collective_id=0, has_side_effects=True, vmem_limit_bytes=60 * 1024 * 1024
        ),
    )(
        inputs,
        query_weight,
        jnp.swapaxes(adapter_down[0], 0, 1),
        adapter_up[0],
        adapter_ids[:, 0],
        new_cache,
        cache_pool,
        page_table,
        lengths,
    )


def solution(mesh):
    in_specs = (
        P(None, ("dec", "ada"), None),
        P(None, "ada"),
        P(("dec", "ada"), None, None),
        P(("dec", "ada"), None, None),
        P(("dec", "ada"), None),
        P(None, ("dec", "ada"), None, None),
        P(("dec", "ada"), None, None, None),
        P(("dec", "ada"), None),
        P(("dec", "ada")),
    )
    out_specs = P(None, ("dec", "ada"), None)
    return jax.shard_map(body, mesh=mesh, in_specs=in_specs, out_specs=out_specs, check_vma=False)
```

```python
import functools
import math

import jax
import jax.numpy as jnp
from jax import lax
from jax.experimental import pallas as pl
from jax.experimental.pallas import tpu as pltpu
from jax.sharding import PartitionSpec as P

HD = 128
CAP = 4
LANES = 128
GROUPS = 1
PARTS = 2
PIECES = GROUPS * PARTS
STRIDE = 6.0
NEGATIVE = -1e30
MESH = pl.DeviceIdType.MESH
F32 = jnp.float32
BF16 = jnp.bfloat16


def nt_dot(a, b):
    return lax.dot_general(a, b, (((1,), (1,)), ((), ())), preferred_element_type=F32)


def iota(shape, axis):
    return lax.broadcasted_iota(jnp.int32, shape, axis)


def kernel(
    n,
    n_dec,
    x_hbm,
    w_hbm,
    down_hbm,
    up_hbm,
    ids_hbm,
    new_hbm,
    pool_hbm,
    table_hbm,
    len_hbm,
    out_ref,
    *scratch,
):
    gathered = scratch[:PIECES]
    (
        x_ref, ids_ref, new_ref, table_ref, len_ref, w_ref, down_ref, up_ref, pages, base, shrink,
        d_send, d_recv, q_send, q_recv, keys, values, result,
        early_sem, w_sem, down_sem, up_sem, pool_sem, pool_send, pool_recv,
        up_send, low_send, across_send, side_send, side_recv, g_recv, ds_sem, dr_sem, qs_sem, qr_sem,
    ) = scratch[PIECES:]
    ada, dec = lax.axis_index("ada"), lax.axis_index("dec")
    steps, rows, width = x_ref.shape
    part = width // PARTS
    span_steps = steps // GROUPS
    block = span_steps * rows
    total = n * block
    head_cols = w_ref.shape[1]
    slots = span_steps * CAP
    span = n // 4
    o, m, c = ada // 4, (ada // 2) % 2, ada % 2
    sibling = ada + 1 - 2 * c
    opposite = ada + 2 - 4 * m
    pool_local = pool_hbm.shape[0]

    def w_copy(k):
        where = pl.ds(k * part, part)
        return pltpu.make_async_copy(w_hbm.at[where], w_ref.at[where], w_sem.at[k])

    down_copy = pltpu.make_async_copy(down_hbm, down_ref, down_sem)
    up_copy = pltpu.make_async_copy(up_hbm, up_ref, up_sem)
    own_pages = pages.at[pl.ds(dec * pool_local, pool_local)]
    pool_copy = pltpu.make_async_copy(pool_hbm, own_pages, pool_sem)

    barrier = pltpu.get_barrier_semaphore()

    def greet(peer):
        pl.semaphore_signal(barrier, inc=1, device_id={"ada": peer}, device_id_type=MESH)

    greet(opposite)
    greet(sibling)
    for side in (1, -1):

        @pl.when((o + side >= 0) & (o + side < span))
        def _():
            greet(ada + 4 * side)

    line_peers = (o >= 1).astype(jnp.int32) + (o + 1 < span).astype(jnp.int32)
    for d in range(1, n_dec):
        pl.semaphore_signal(
            barrier, inc=1, device_id={"dec": lax.rem(dec + d, n_dec)}, device_id_type=MESH
        )
    early = [
        pltpu.make_async_copy(source, target, early_sem.at[i])
        for i, (source, target) in enumerate(
            [(x_hbm, x_ref), (ids_hbm, ids_ref), (new_hbm, new_ref), (table_hbm, table_ref), (len_hbm, len_ref)]
        )
    ]
    for copy in early:
        copy.start()
    down_copy.start()
    for k in range(PARTS):
        w_copy(k).start()
    up_copy.start()
    pool_copy.start()

    early[0].wait()
    early[1].wait()
    row_of = iota((block, LANES), 0) % rows
    id_block = jnp.zeros((block, LANES), F32)
    for r in range(rows):
        id_block = jnp.where(row_of == r, ids_ref[r].astype(F32), id_block)
    gathered[0][ada, :, part : part + LANES] = id_block.astype(BF16)
    for g in range(GROUPS):
        mine = jnp.concatenate(
            [x_ref[g * span_steps + t].astype(F32) for t in range(span_steps)], axis=0
        ).astype(BF16)
        for k in range(PARTS):
            gathered[g * PARTS + k][ada, :, 0:part] = mine[:, k * part : (k + 1) * part]
    pl.semaphore_wait(barrier, line_peers + 2 + n_dec - 1)

    def relay(k, source, send_sem, peer):
        return pltpu.make_async_remote_copy(
            src_ref=gathered[k].at[source],
            dst_ref=gathered[k].at[source],
            send_sem=send_sem,
            recv_sem=g_recv.at[k, source],
            device_id={"ada": peer},
            device_id_type=MESH,
        )

    def arrived(k, source):
        relay(k, source, across_send.at[k, 0], opposite).wait_recv()

    def upward(k, line):
        return relay(k, line * 4 + m * 2 + c, up_send.at[k, line], ada + 4)

    def downward(k, line):
        return relay(k, line * 4 + m * 2 + c, low_send.at[k, line], ada - 4)

    def across(k, line):
        return relay(k, line * 4 + m * 2 + c, across_send.at[k, line], opposite)

    def sideways(k, line, column):
        source = line * 4 + column * 2 + c
        return pltpu.make_async_remote_copy(
            src_ref=gathered[k].at[source],
            dst_ref=gathered[k].at[source],
            send_sem=side_send.at[k],
            recv_sem=side_recv.at[k],
            device_id={"ada": sibling},
            device_id_type=MESH,
        )

    def all_sideways(k):
        half = gathered[k].at[pl.ds(0, n // 2)]
        return pltpu.make_async_remote_copy(
            src_ref=half,
            dst_ref=half,
            send_sem=side_send.at[k],
            recv_sem=side_recv.at[k],
            device_id={"ada": sibling},
            device_id_type=MESH,
        )

    def send_own(k):
        @pl.when(o < span - 1)
        def _():
            upward(k, o).start()

        @pl.when(o > 0)
        def _():
            downward(k, o).start()

        across(k, o).start()
        sideways(k, o, m).start()

    def line_event(k, distance):
        below, above = o - distance, o + distance

        @pl.when(below >= 0)
        def _():
            arrived(k, below * 4 + m * 2 + c)

            @pl.when(o < span - 1)
            def _():
                upward(k, below).start()

            across(k, below).start()
            sideways(k, below, m).start()

        @pl.when(above < span)
        def _():
            arrived(k, above * 4 + m * 2 + c)

            @pl.when(o > 0)
            def _():
                downward(k, above).start()

            across(k, above).start()
            sideways(k, above, m).start()

    def across_event(k, distance):
        other = 1 - m
        below, above = o - distance, o + distance

        @pl.when(below >= 0)
        def _():
            arrived(k, below * 4 + other * 2 + c)
            sideways(k, below, other).start()

        if distance:

            @pl.when(above < span)
            def _():
                arrived(k, above * 4 + other * 2 + c)
                sideways(k, above, other).start()

    def side_wave(k):
        all_sideways(k).wait_recv()

    def piece_rows(g, k):
        held = gathered[g * PARTS + k]
        return held[:, :, 0:part].reshape(total, part)

    def add_shrink(g):
        for k in range(PARTS):
            term = nt_dot(piece_rows(g, k), down_ref[:, k * part : (k + 1) * part])
            shrink[g] = term if k == 0 else shrink[g] + term

    def add_base(g):
        for k in range(PARTS):
            term = jnp.dot(
                piece_rows(g, k),
                w_ref[k * part : (k + 1) * part, :],
                preferred_element_type=F32,
            )
            base[g] = term if k == 0 else base[g] + term

    def pool_send_copy(d):
        return pltpu.make_async_remote_copy(
            src_ref=pool_hbm,
            dst_ref=own_pages,
            send_sem=pool_send.at[d],
            recv_sem=pool_recv.at[dec],
            device_id={"dec": lax.rem(dec + d, n_dec)},
            device_id_type=MESH,
        )

    def pool_arrived(owner):
        pltpu.make_async_remote_copy(
            src_ref=pool_hbm,
            dst_ref=pages.at[pl.ds(owner * pool_local, pool_local)],
            send_sem=pool_send.at[1],
            recv_sem=pool_recv.at[owner],
            device_id={"dec": lax.rem(dec + 1, n_dec)},
            device_id_type=MESH,
        ).wait_recv()

    def slot_masks():
        id_col = jnp.concatenate(
            [gathered[0][source, :, part : part + LANES].astype(F32) for source in range(n)], axis=0
        )[:, 0:1]
        at_row, at_lane = iota((total, total), 0), iota((total, total), 1)
        id_row = jnp.sum(jnp.where(at_row == at_lane, id_col, 0.0), axis=0, keepdims=True)
        same = id_col == id_row
        row_rank = at_row // block * rows + at_row % rows
        lane_rank = at_lane // block * rows + at_lane % rows
        count_row = jnp.sum(
            jnp.where(same & (row_rank < lane_rank) & (at_row % block < rows), 1.0, 0.0),
            axis=0,
            keepdims=True,
        )
        slot, lane = iota((slots, total), 0), iota((slots, total), 1)
        pick = jnp.where(
            (slot // CAP == lane % block // rows)
            & (id_row == ada.astype(F32))
            & (count_row == (slot % CAP).astype(F32)),
            1.0,
            0.0,
        ).astype(BF16)

        def spread_mask():
            count_col = jnp.sum(
                jnp.where(same & (lane_rank < row_rank) & (at_lane % block < rows), 1.0, 0.0),
                axis=1,
                keepdims=True,
            )
            row, place = iota((total, n * slots), 0), iota((total, n * slots), 1)
            spread = jnp.where(
                (row % block // rows == place % slots // CAP)
                & (id_col == (place // slots).astype(F32))
                & (count_col == (place % CAP).astype(F32)),
                1.0,
                0.0,
            ).astype(BF16)
            return spread

        return pick, spread_mask

    entries, page = table_ref.shape[1], pages.shape[2]
    cached = rows * entries * page
    fresh_rows = steps * rows
    kv_heads = keys.shape[1] // HD
    heads = width // HD
    group = heads // kv_heads
    count = keys.shape[0]

    def key_mask(g):
        query_at, key_at = iota((heads * block, count), 0), iota((heads * block, count), 1)
        query_step, query_row = query_at % block // rows + g * span_steps, query_at % rows
        limit = jnp.zeros((heads * block, count), jnp.int32)
        for r in range(rows):
            limit = jnp.where(query_row == r, len_ref[r], limit)
        in_cache = (
            (key_at < cached)
            & (key_at // (entries * page) == query_row)
            & (key_at % (entries * page) < limit)
        )
        late = key_at - cached
        in_new = (late >= 0) & (late % rows == query_row) & (late // rows <= query_step)
        return in_cache | in_new

    def delta_of(g, chosen, target):
        columns = pl.ds(pl.multiple_of(target * head_cols, head_cols), head_cols)
        return jnp.dot(chosen, up_ref[:, columns], preferred_element_type=F32).astype(BF16)

    def d_copy(g, source, target):
        return pltpu.make_async_remote_copy(
            src_ref=d_send.at[g, target],
            dst_ref=d_recv.at[g, source],
            send_sem=ds_sem.at[g],
            recv_sem=dr_sem.at[g],
            device_id={"ada": target},
            device_id_type=MESH,
        )

    def q_copy(g, source, target):
        return pltpu.make_async_remote_copy(
            src_ref=q_send.at[g, target],
            dst_ref=q_recv.at[g, source],
            send_sem=qs_sem.at[g],
            recv_sem=qr_sem.at[g],
            device_id={"ada": target},
            device_id_type=MESH,
        )

    def others(sent, received, send_sem, recv_sem, g):
        return pltpu.make_async_remote_copy(
            src_ref=sent.at[g, pl.ds(0, n - 1)],
            dst_ref=received.at[g, pl.ds(0, n - 1)],
            send_sem=send_sem.at[g],
            recv_sem=recv_sem.at[g],
            device_id={"ada": sibling},
            device_id_type=MESH,
        )

    def all_deltas(g):
        return others(d_send, d_recv, ds_sem, dr_sem, g)

    def all_queries(g):
        return others(q_send, q_recv, qs_sem, qr_sem, g)

    order = range(1, n)
    targets = [lax.rem(ada + d, n) for d in order]

    def send_delta(g):
        chosen = jnp.dot(pick, shrink[g].astype(BF16), preferred_element_type=F32).astype(BF16)
        for i, target in enumerate(targets):
            d_send[g, target] = delta_of(g, chosen, target)
            if i > 0:
                d_copy(g, ada, targets[i - 1]).start()
        d_recv[g, ada] = delta_of(g, chosen, ada)
        d_copy(g, ada, targets[-1]).start()

    def send_query(g):
        all_deltas(g).wait_recv()
        received = d_recv[g].astype(F32).reshape(n * slots, head_cols).astype(BF16)
        update = jnp.dot(spread, received, preferred_element_type=F32)
        query = base[g] + update
        for source in range(n):
            q_send[g, source] = query[source * block : (source + 1) * block].astype(BF16)
        for target in targets:
            q_copy(g, ada, target).start()
        q_recv[g, ada] = q_send[g, ada]

    scale = 1.0 / math.sqrt(HD)
    per_source = head_cols // HD

    def attend(g, allowed):
        all_queries(g).wait_recv()
        scores = []
        for h in range(kv_heads):
            parts = []
            for j in range(group):
                head = h * group + j
                first = head % per_source * HD
                parts.append(q_recv[g, head // per_source, :, first : first + HD].astype(F32))
            query = jnp.concatenate(parts, axis=0).astype(BF16)
            scores.append(nt_dot(query, keys[:, h * HD : (h + 1) * HD]))
        scores = jnp.where(allowed, jnp.concatenate(scores, axis=0) * scale, NEGATIVE)
        top = jnp.max(scores, axis=1, keepdims=True)
        weights = jnp.where(allowed, jnp.exp(scores - top), 0.0)
        denominator = jnp.sum(weights, axis=1, keepdims=True)
        high = weights.astype(BF16)
        low = (weights - high.astype(F32)).astype(BF16)
        height = group * block
        for h in range(kv_heads):
            at, lanes = slice(h * height, (h + 1) * height), slice(h * HD, (h + 1) * HD)
            both = jnp.dot(
                jnp.concatenate([high[at], low[at]], axis=0),
                values[:, lanes],
                preferred_element_type=F32,
            )
            attended = (both[:height] + both[height:]) / denominator[at]
            for j in range(group):
                first = (h * group + j) * HD
                result[g, :, first : first + HD] = attended[j * block : (j + 1) * block]
        for t in range(span_steps):
            out_ref[g * span_steps + t] = result[g, t * rows : (t + 1) * rows, :].astype(BF16)

    events = []
    for p in range(PIECES):
        events.append((p * 1.0, 0, p, 0))
        for distance in range(1, span):
            events.append((p + STRIDE * distance, 1, p, distance))
        for distance in range(span):
            events.append((p + STRIDE * (distance + 1), 2, p, distance))
        events.append((p + STRIDE * (span + 1), 3, p, 0))
    events.sort()
    pick = spread_mask = None
    for _, kind, p, distance in events:
        if kind == 0:
            send_own(p)
            if p == min(1, PIECES - 1):
                for d in range(1, n_dec):
                    pool_send_copy(d).start()
        elif kind == 1:
            line_event(p, distance)
        elif kind == 2:
            across_event(p, distance)
        else:
            side_wave(p)
            if p == 0:
                pick, spread_mask = slot_masks()
                down_copy.wait()
                up_copy.wait()
            if p % PARTS == PARTS - 1:
                g = p // PARTS
                add_shrink(g)
                send_delta(g)
                if g == 0:
                    for k in range(PARTS):
                        w_copy(k).wait()
                if g == GROUPS - 1:
                    for i in range(g + 1):
                        add_base(i)

    for copy in early[2:]:
        copy.wait()
    spread = spread_mask()
    masks = [key_mask(g) for g in range(GROUPS)]
    pool_copy.wait()
    for d in range(1, n_dec):
        pool_arrived(lax.rem(dec + d, n_dec))
    for r in range(rows):
        for j in range(entries):
            held = pages[table_ref[r, j]]
            first = (r * entries + j) * page
            keys[first : first + page, :] = held[0]
            values[first : first + page, :] = held[1]
    fresh = [new_ref[u, r].astype(F32) for u in range(steps) for r in range(rows)]
    empty = jnp.zeros((keys.shape[0] - cached - fresh_rows, keys.shape[1]), F32)
    keys[cached:, :] = jnp.concatenate([f[0:1] for f in fresh] + [empty], axis=0).astype(BF16)
    values[cached:, :] = jnp.concatenate([f[1:2] for f in fresh] + [empty], axis=0).astype(BF16)

    for k in range(PIECES):
        all_sideways(k).wait_send()
        for line in range(span):
            across(k, line).wait_send()

            @pl.when((line <= o) & (o < span - 1))
            def _():
                upward(k, line).wait_send()

            @pl.when((line >= o) & (o > 0))
            def _():
                downward(k, line).wait_send()

    for d in range(1, n_dec):
        pool_send_copy(d).wait_send()
    for g in range(GROUPS):
        send_query(g)
    for g in range(GROUPS):
        all_deltas(g).wait_send()
    for g in range(GROUPS):
        attend(g, masks[g])

    for g in range(GROUPS):
        all_queries(g).wait_send()


def body(
    inputs,
    query_weight,
    adapter_down,
    adapter_up,
    adapter_ids,
    new_cache,
    cache_pool,
    page_table,
    lengths,
):
    n, n_dec = lax.axis_size("ada"), lax.axis_size("dec")
    steps, rows, width = inputs.shape
    held, _, rank = adapter_down.shape
    assert held == 1 and n % 4 == 0
    head_cols = query_weight.shape[1]
    block, slots, span = steps // GROUPS * rows, steps // GROUPS * CAP, n // 4
    part = width // PARTS
    pool_local, _, page, kv_width = cache_pool.shape
    count = -(-(rows * page_table.shape[1] * page + steps * rows) // 16) * 16
    dma = pltpu.SemaphoreType.DMA
    vmem, hbm = pl.BlockSpec(memory_space=pltpu.VMEM), pl.BlockSpec(memory_space=pl.ANY)
    scratch = [
        pltpu.VMEM((n, block, part + (LANES if k == 0 else 0)), BF16) for k in range(PIECES)
    ] + [
        pltpu.VMEM(inputs.shape, BF16),
        pltpu.SMEM((rows,), jnp.int32),
        pltpu.VMEM(new_cache.shape, BF16),
        pltpu.SMEM(page_table.shape, jnp.int32),
        pltpu.SMEM(lengths.shape, jnp.int32),
        pltpu.VMEM((width, head_cols), BF16),
        pltpu.VMEM((rank, width), BF16),
        pltpu.VMEM((rank, width), BF16),
        pltpu.VMEM((n_dec * pool_local, 2, page, kv_width), BF16),
        pltpu.VMEM((GROUPS, n * block, head_cols), F32),
        pltpu.VMEM((GROUPS, n * block, rank), F32),
        pltpu.VMEM((GROUPS, n, slots, head_cols), BF16),
        pltpu.VMEM((GROUPS, n, slots, head_cols), BF16),
        pltpu.VMEM((GROUPS, n, block, head_cols), BF16),
        pltpu.VMEM((GROUPS, n, block, head_cols), BF16),
        pltpu.VMEM((count, kv_width), BF16),
        pltpu.VMEM((count, kv_width), BF16),
        pltpu.VMEM((GROUPS, block, width), F32),
        dma((5,)),
        dma((PARTS,)),
        dma,
        dma,
        dma,
        dma((n_dec,)),
        dma((n_dec,)),
        dma((PIECES, span)),
        dma((PIECES, span)),
        dma((PIECES, span)),
        dma((PIECES,)),
        dma((PIECES,)),
        dma((PIECES, n)),
        dma((GROUPS,)),
        dma((GROUPS,)),
        dma((GROUPS,)),
        dma((GROUPS,)),
    ]
    return pl.pallas_call(
        functools.partial(kernel, n, n_dec),
        out_shape=pltpu.VMEM((steps, rows, width), BF16),
        in_specs=[hbm] * 9,
        out_specs=vmem,
        scratch_shapes=scratch,
        compiler_params=pltpu.CompilerParams(
            collective_id=0, has_side_effects=True, vmem_limit_bytes=60 * 1024 * 1024
        ),
    )(
        inputs,
        query_weight,
        jnp.swapaxes(adapter_down[0], 0, 1),
        adapter_up[0],
        adapter_ids[:, 0],
        new_cache,
        cache_pool,
        page_table,
        lengths,
    )


def solution(mesh):
    in_specs = (
        P(None, ("dec", "ada"), None),
        P(None, "ada"),
        P(("dec", "ada"), None, None),
        P(("dec", "ada"), None, None),
        P(("dec", "ada"), None),
        P(None, ("dec", "ada"), None, None),
        P(("dec", "ada"), None, None, None),
        P(("dec", "ada"), None),
        P(("dec", "ada")),
    )
    out_specs = P(None, ("dec", "ada"), None)
    return jax.shard_map(body, mesh=mesh, in_specs=in_specs, out_specs=out_specs, check_vma=False)
```

```python
import functools
import math

import jax
import jax.numpy as jnp
from jax import lax
from jax.experimental import pallas as pl
from jax.experimental.pallas import tpu as pltpu
from jax.sharding import PartitionSpec as P

HD = 128
CAP = 4
LANES = 128
GROUPS = 1
PARTS = 2
PIECES = GROUPS * PARTS
STRIDE = 6.0
NEGATIVE = -1e30
MESH = pl.DeviceIdType.MESH
F32 = jnp.float32
BF16 = jnp.bfloat16


def nt_dot(a, b):
    return lax.dot_general(a, b, (((1,), (1,)), ((), ())), preferred_element_type=F32)


def iota(shape, axis):
    return lax.broadcasted_iota(jnp.int32, shape, axis)


def kernel(
    n,
    n_dec,
    x_hbm,
    w_hbm,
    down_hbm,
    up_hbm,
    ids_hbm,
    new_hbm,
    pool_hbm,
    table_hbm,
    len_hbm,
    out_ref,
    *scratch,
):
    gathered = scratch[:PIECES]
    (
        x_ref, ids_ref, new_ref, table_ref, len_ref, w_ref, down_ref, up_ref, pages, base, shrink,
        d_send, d_recv, q_send, q_recv, keys, values, result,
        early_sem, w_sem, down_sem, up_sem, pool_sem, pool_send, pool_recv,
        up_send, low_send, across_send, side_send, side_recv, g_recv, ds_sem, dr_sem, qs_sem, qr_sem,
    ) = scratch[PIECES:]
    ada, dec = lax.axis_index("ada"), lax.axis_index("dec")
    steps, rows, width = x_ref.shape
    part = width // PARTS
    span_steps = steps // GROUPS
    block = span_steps * rows
    total = n * block
    head_cols = w_ref.shape[1]
    slots = span_steps * CAP
    span = n // 4
    o, m, c = ada // 4, (ada // 2) % 2, ada % 2
    sibling = ada + 1 - 2 * c
    opposite = ada + 2 - 4 * m
    pool_local = pool_hbm.shape[0]

    def w_copy(k):
        where = pl.ds(k * part, part)
        return pltpu.make_async_copy(w_hbm.at[where], w_ref.at[where], w_sem.at[k])

    down_copy = pltpu.make_async_copy(down_hbm, down_ref, down_sem)
    up_copy = pltpu.make_async_copy(up_hbm, up_ref, up_sem)
    own_pages = pages.at[pl.ds(dec * pool_local, pool_local)]
    pool_copy = pltpu.make_async_copy(pool_hbm, own_pages, pool_sem)

    barrier = pltpu.get_barrier_semaphore()

    def greet(peer):
        pl.semaphore_signal(barrier, inc=1, device_id={"ada": peer}, device_id_type=MESH)

    greet(opposite)
    greet(sibling)
    for side in (1, -1):

        @pl.when((o + side >= 0) & (o + side < span))
        def _():
            greet(ada + 4 * side)

    line_peers = (o >= 1).astype(jnp.int32) + (o + 1 < span).astype(jnp.int32)
    for d in range(1, n_dec):
        pl.semaphore_signal(
            barrier, inc=1, device_id={"dec": lax.rem(dec + d, n_dec)}, device_id_type=MESH
        )
    early = [
        pltpu.make_async_copy(source, target, early_sem.at[i])
        for i, (source, target) in enumerate(
            [(x_hbm, x_ref), (ids_hbm, ids_ref), (new_hbm, new_ref), (table_hbm, table_ref), (len_hbm, len_ref)]
        )
    ]
    for copy in early:
        copy.start()
    down_copy.start()
    for k in range(PARTS):
        w_copy(k).start()
    up_copy.start()
    pool_copy.start()

    early[0].wait()
    early[1].wait()
    row_of = iota((block, LANES), 0) % rows
    id_block = jnp.zeros((block, LANES), F32)
    for r in range(rows):
        id_block = jnp.where(row_of == r, ids_ref[r].astype(F32), id_block)
    gathered[0][ada, :, part : part + LANES] = id_block.astype(BF16)
    for g in range(GROUPS):
        mine = jnp.concatenate(
            [x_ref[g * span_steps + t].astype(F32) for t in range(span_steps)], axis=0
        ).astype(BF16)
        for k in range(PARTS):
            gathered[g * PARTS + k][ada, :, 0:part] = mine[:, k * part : (k + 1) * part]
    pl.semaphore_wait(barrier, line_peers + 2 + n_dec - 1)

    def relay(k, source, send_sem, peer):
        return pltpu.make_async_remote_copy(
            src_ref=gathered[k].at[source],
            dst_ref=gathered[k].at[source],
            send_sem=send_sem,
            recv_sem=g_recv.at[k, source],
            device_id={"ada": peer},
            device_id_type=MESH,
        )

    def arrived(k, source):
        relay(k, source, across_send.at[k, 0], opposite).wait_recv()

    def upward(k, line):
        return relay(k, line * 4 + m * 2 + c, up_send.at[k, line], ada + 4)

    def downward(k, line):
        return relay(k, line * 4 + m * 2 + c, low_send.at[k, line], ada - 4)

    def across(k, line):
        return relay(k, line * 4 + m * 2 + c, across_send.at[k, line], opposite)

    def sideways(k, line, column):
        source = line * 4 + column * 2 + c
        return pltpu.make_async_remote_copy(
            src_ref=gathered[k].at[source],
            dst_ref=gathered[k].at[source],
            send_sem=side_send.at[k],
            recv_sem=side_recv.at[k],
            device_id={"ada": sibling},
            device_id_type=MESH,
        )

    def all_sideways(k):
        half = gathered[k].at[pl.ds(0, n // 2)]
        return pltpu.make_async_remote_copy(
            src_ref=half,
            dst_ref=half,
            send_sem=side_send.at[k],
            recv_sem=side_recv.at[k],
            device_id={"ada": sibling},
            device_id_type=MESH,
        )

    def send_own(k):
        @pl.when(o < span - 1)
        def _():
            upward(k, o).start()

        @pl.when(o > 0)
        def _():
            downward(k, o).start()

        across(k, o).start()
        sideways(k, o, m).start()

    def line_event(k, distance):
        below, above = o - distance, o + distance

        @pl.when(below >= 0)
        def _():
            arrived(k, below * 4 + m * 2 + c)

            @pl.when(o < span - 1)
            def _():
                upward(k, below).start()

            across(k, below).start()
            sideways(k, below, m).start()

        @pl.when(above < span)
        def _():
            arrived(k, above * 4 + m * 2 + c)

            @pl.when(o > 0)
            def _():
                downward(k, above).start()

            across(k, above).start()
            sideways(k, above, m).start()

    def across_event(k, distance):
        other = 1 - m
        below, above = o - distance, o + distance

        @pl.when(below >= 0)
        def _():
            arrived(k, below * 4 + other * 2 + c)
            sideways(k, below, other).start()

        if distance:

            @pl.when(above < span)
            def _():
                arrived(k, above * 4 + other * 2 + c)
                sideways(k, above, other).start()

    def side_wave(k):
        all_sideways(k).wait_recv()

    def piece_rows(g, k):
        held = gathered[g * PARTS + k]
        return held[:, :, 0:part].reshape(total, part)

    def add_shrink(g):
        for k in range(PARTS):
            term = nt_dot(piece_rows(g, k), down_ref[:, k * part : (k + 1) * part])
            shrink[g] = term if k == 0 else shrink[g] + term

    def add_base(g):
        for k in range(PARTS):
            term = jnp.dot(
                piece_rows(g, k),
                w_ref[k * part : (k + 1) * part, :],
                preferred_element_type=F32,
            )
            base[g] = term if k == 0 else base[g] + term

    def pool_send_copy(d):
        return pltpu.make_async_remote_copy(
            src_ref=pool_hbm,
            dst_ref=own_pages,
            send_sem=pool_send.at[d],
            recv_sem=pool_recv.at[dec],
            device_id={"dec": lax.rem(dec + d, n_dec)},
            device_id_type=MESH,
        )

    def pool_arrived(owner):
        pltpu.make_async_remote_copy(
            src_ref=pool_hbm,
            dst_ref=pages.at[pl.ds(owner * pool_local, pool_local)],
            send_sem=pool_send.at[1],
            recv_sem=pool_recv.at[owner],
            device_id={"dec": lax.rem(dec + 1, n_dec)},
            device_id_type=MESH,
        ).wait_recv()

    def slot_masks():
        id_col = jnp.concatenate(
            [gathered[0][source, :, part : part + LANES].astype(F32) for source in range(n)], axis=0
        )[:, 0:1]
        at_row, at_lane = iota((total, total), 0), iota((total, total), 1)
        id_row = jnp.sum(jnp.where(at_row == at_lane, id_col, 0.0), axis=0, keepdims=True)
        same = id_col == id_row
        row_rank = at_row // block * rows + at_row % rows
        lane_rank = at_lane // block * rows + at_lane % rows
        count_row = jnp.sum(
            jnp.where(same & (row_rank < lane_rank) & (at_row % block < rows), 1.0, 0.0),
            axis=0,
            keepdims=True,
        )
        slot, lane = iota((slots, total), 0), iota((slots, total), 1)
        pick = jnp.where(
            (slot // CAP == lane % block // rows)
            & (id_row == ada.astype(F32))
            & (count_row == (slot % CAP).astype(F32)),
            1.0,
            0.0,
        ).astype(BF16)

        def spread_mask():
            count_col = jnp.sum(
                jnp.where(same & (lane_rank < row_rank) & (at_lane % block < rows), 1.0, 0.0),
                axis=1,
                keepdims=True,
            )
            row, place = iota((total, n * slots), 0), iota((total, n * slots), 1)
            spread = jnp.where(
                (row % block // rows == place % slots // CAP)
                & (id_col == (place // slots).astype(F32))
                & (count_col == (place % CAP).astype(F32)),
                1.0,
                0.0,
            ).astype(BF16)
            return spread

        return pick, spread_mask

    entries, page = table_ref.shape[1], pages.shape[2]
    cached = rows * entries * page
    fresh_rows = steps * rows
    kv_heads = keys.shape[1] // HD
    heads = width // HD
    group = heads // kv_heads
    count = keys.shape[0]

    def key_mask(g):
        query_at, key_at = iota((heads * block, count), 0), iota((heads * block, count), 1)
        query_step, query_row = query_at % block // rows + g * span_steps, query_at % rows
        limit = jnp.zeros((heads * block, count), jnp.int32)
        for r in range(rows):
            limit = jnp.where(query_row == r, len_ref[r], limit)
        in_cache = (
            (key_at < cached)
            & (key_at // (entries * page) == query_row)
            & (key_at % (entries * page) < limit)
        )
        late = key_at - cached
        in_new = (late >= 0) & (late % rows == query_row) & (late // rows <= query_step)
        return in_cache | in_new

    def delta_of(g, chosen, target):
        columns = pl.ds(pl.multiple_of(target * head_cols, head_cols), head_cols)
        return jnp.dot(chosen, up_ref[:, columns], preferred_element_type=F32).astype(BF16)

    def d_copy(g, source, target):
        return pltpu.make_async_remote_copy(
            src_ref=d_send.at[g, target],
            dst_ref=d_recv.at[g, source],
            send_sem=ds_sem.at[g],
            recv_sem=dr_sem.at[g],
            device_id={"ada": target},
            device_id_type=MESH,
        )

    def q_copy(g, source, target):
        return pltpu.make_async_remote_copy(
            src_ref=q_send.at[g, target],
            dst_ref=q_recv.at[g, source],
            send_sem=qs_sem.at[g],
            recv_sem=qr_sem.at[g],
            device_id={"ada": target},
            device_id_type=MESH,
        )

    def others(sent, received, send_sem, recv_sem, g):
        return pltpu.make_async_remote_copy(
            src_ref=sent.at[g, pl.ds(0, n - 1)],
            dst_ref=received.at[g, pl.ds(0, n - 1)],
            send_sem=send_sem.at[g],
            recv_sem=recv_sem.at[g],
            device_id={"ada": sibling},
            device_id_type=MESH,
        )

    def all_deltas(g):
        return others(d_send, d_recv, ds_sem, dr_sem, g)

    def all_queries(g):
        return others(q_send, q_recv, qs_sem, qr_sem, g)

    order = range(1, n)
    targets = [lax.rem(ada + d, n) for d in order]

    def send_delta(g):
        chosen = jnp.dot(pick, shrink[g].astype(BF16), preferred_element_type=F32).astype(BF16)
        for i, target in enumerate(targets):
            d_send[g, target] = delta_of(g, chosen, target)
            if i > 0:
                d_copy(g, ada, targets[i - 1]).start()
        d_recv[g, ada] = delta_of(g, chosen, ada)
        d_copy(g, ada, targets[-1]).start()

    def send_query(g):
        all_deltas(g).wait_recv()
        received = d_recv[g].reshape(n * slots, head_cols)
        update = jnp.dot(spread, received, preferred_element_type=F32)
        query = base[g] + update
        q_send[g] = query.reshape(n, block, head_cols).astype(BF16)
        for target in targets:
            q_copy(g, ada, target).start()
        q_recv[g, ada] = q_send[g, ada]

    scale = 1.0 / math.sqrt(HD)
    per_source = head_cols // HD

    def attend(g, allowed):
        all_queries(g).wait_recv()
        scores = []
        for h in range(kv_heads):
            parts = []
            for j in range(group):
                head = h * group + j
                first = head % per_source * HD
                parts.append(q_recv[g, head // per_source, :, first : first + HD].astype(F32))
            query = jnp.concatenate(parts, axis=0).astype(BF16)
            scores.append(nt_dot(query, keys[:, h * HD : (h + 1) * HD]))
        scores = jnp.where(allowed, jnp.concatenate(scores, axis=0) * scale, NEGATIVE)
        top = jnp.max(scores, axis=1, keepdims=True)
        weights = jnp.where(allowed, jnp.exp(scores - top), 0.0)
        denominator = jnp.sum(weights, axis=1, keepdims=True)
        high = weights.astype(BF16)
        low = (weights - high.astype(F32)).astype(BF16)
        height = group * block
        for h in range(kv_heads):
            at, lanes = slice(h * height, (h + 1) * height), slice(h * HD, (h + 1) * HD)
            both = jnp.dot(
                jnp.concatenate([high[at], low[at]], axis=0),
                values[:, lanes],
                preferred_element_type=F32,
            )
            attended = (both[:height] + both[height:]) / denominator[at]
            for j in range(group):
                first = (h * group + j) * HD
                result[g, :, first : first + HD] = attended[j * block : (j + 1) * block]
        for t in range(span_steps):
            out_ref[g * span_steps + t] = result[g, t * rows : (t + 1) * rows, :].astype(BF16)

    events = []
    for p in range(PIECES):
        events.append((p * 1.0, 0, p, 0))
        for distance in range(1, span):
            events.append((p + STRIDE * distance, 1, p, distance))
        for distance in range(span):
            events.append((p + STRIDE * (distance + 1), 2, p, distance))
        events.append((p + STRIDE * (span + 1), 3, p, 0))
    events.sort()
    pick = spread_mask = None
    for _, kind, p, distance in events:
        if kind == 0:
            send_own(p)
            if p == min(1, PIECES - 1):
                for d in range(1, n_dec):
                    pool_send_copy(d).start()
        elif kind == 1:
            line_event(p, distance)
        elif kind == 2:
            across_event(p, distance)
        else:
            side_wave(p)
            if p == 0:
                pick, spread_mask = slot_masks()
                down_copy.wait()
                up_copy.wait()
            if p % PARTS == PARTS - 1:
                g = p // PARTS
                add_shrink(g)
                send_delta(g)
                if g == 0:
                    for k in range(PARTS):
                        w_copy(k).wait()
                if g == GROUPS - 1:
                    for i in range(g + 1):
                        add_base(i)

    for copy in early[2:]:
        copy.wait()
    spread = spread_mask()
    masks = [key_mask(g) for g in range(GROUPS)]
    pool_copy.wait()
    for d in range(1, n_dec):
        pool_arrived(lax.rem(dec + d, n_dec))
    for r in range(rows):
        for j in range(entries):
            held = pages[table_ref[r, j]]
            first = (r * entries + j) * page
            keys[first : first + page, :] = held[0]
            values[first : first + page, :] = held[1]
    fresh = [new_ref[u, r].astype(F32) for u in range(steps) for r in range(rows)]
    empty = jnp.zeros((keys.shape[0] - cached - fresh_rows, keys.shape[1]), F32)
    keys[cached:, :] = jnp.concatenate([f[0:1] for f in fresh] + [empty], axis=0).astype(BF16)
    values[cached:, :] = jnp.concatenate([f[1:2] for f in fresh] + [empty], axis=0).astype(BF16)

    for k in range(PIECES):
        all_sideways(k).wait_send()
        for line in range(span):
            across(k, line).wait_send()

            @pl.when((line <= o) & (o < span - 1))
            def _():
                upward(k, line).wait_send()

            @pl.when((line >= o) & (o > 0))
            def _():
                downward(k, line).wait_send()

    for d in range(1, n_dec):
        pool_send_copy(d).wait_send()
    for g in range(GROUPS):
        send_query(g)
    for g in range(GROUPS):
        all_deltas(g).wait_send()
    for g in range(GROUPS):
        attend(g, masks[g])

    for g in range(GROUPS):
        all_queries(g).wait_send()


def body(
    inputs,
    query_weight,
    adapter_down,
    adapter_up,
    adapter_ids,
    new_cache,
    cache_pool,
    page_table,
    lengths,
):
    n, n_dec = lax.axis_size("ada"), lax.axis_size("dec")
    steps, rows, width = inputs.shape
    held, _, rank = adapter_down.shape
    assert held == 1 and n % 4 == 0
    head_cols = query_weight.shape[1]
    block, slots, span = steps // GROUPS * rows, steps // GROUPS * CAP, n // 4
    part = width // PARTS
    pool_local, _, page, kv_width = cache_pool.shape
    count = -(-(rows * page_table.shape[1] * page + steps * rows) // 16) * 16
    dma = pltpu.SemaphoreType.DMA
    vmem, hbm = pl.BlockSpec(memory_space=pltpu.VMEM), pl.BlockSpec(memory_space=pl.ANY)
    scratch = [
        pltpu.VMEM((n, block, part + (LANES if k == 0 else 0)), BF16) for k in range(PIECES)
    ] + [
        pltpu.VMEM(inputs.shape, BF16),
        pltpu.SMEM((rows,), jnp.int32),
        pltpu.VMEM(new_cache.shape, BF16),
        pltpu.SMEM(page_table.shape, jnp.int32),
        pltpu.SMEM(lengths.shape, jnp.int32),
        pltpu.VMEM((width, head_cols), BF16),
        pltpu.VMEM((rank, width), BF16),
        pltpu.VMEM((rank, width), BF16),
        pltpu.VMEM((n_dec * pool_local, 2, page, kv_width), BF16),
        pltpu.VMEM((GROUPS, n * block, head_cols), F32),
        pltpu.VMEM((GROUPS, n * block, rank), F32),
        pltpu.VMEM((GROUPS, n, slots, head_cols), BF16),
        pltpu.VMEM((GROUPS, n, slots, head_cols), BF16),
        pltpu.VMEM((GROUPS, n, block, head_cols), BF16),
        pltpu.VMEM((GROUPS, n, block, head_cols), BF16),
        pltpu.VMEM((count, kv_width), BF16),
        pltpu.VMEM((count, kv_width), BF16),
        pltpu.VMEM((GROUPS, block, width), F32),
        dma((5,)),
        dma((PARTS,)),
        dma,
        dma,
        dma,
        dma((n_dec,)),
        dma((n_dec,)),
        dma((PIECES, span)),
        dma((PIECES, span)),
        dma((PIECES, span)),
        dma((PIECES,)),
        dma((PIECES,)),
        dma((PIECES, n)),
        dma((GROUPS,)),
        dma((GROUPS,)),
        dma((GROUPS,)),
        dma((GROUPS,)),
    ]
    return pl.pallas_call(
        functools.partial(kernel, n, n_dec),
        out_shape=pltpu.VMEM((steps, rows, width), BF16),
        in_specs=[hbm] * 9,
        out_specs=vmem,
        scratch_shapes=scratch,
        compiler_params=pltpu.CompilerParams(
            collective_id=0, has_side_effects=True, vmem_limit_bytes=60 * 1024 * 1024
        ),
    )(
        inputs,
        query_weight,
        jnp.swapaxes(adapter_down[0], 0, 1),
        adapter_up[0],
        adapter_ids[:, 0],
        new_cache,
        cache_pool,
        page_table,
        lengths,
    )


def solution(mesh):
    in_specs = (
        P(None, ("dec", "ada"), None),
        P(None, "ada"),
        P(("dec", "ada"), None, None),
        P(("dec", "ada"), None, None),
        P(("dec", "ada"), None),
        P(None, ("dec", "ada"), None, None),
        P(("dec", "ada"), None, None, None),
        P(("dec", "ada"), None),
        P(("dec", "ada")),
    )
    out_specs = P(None, ("dec", "ada"), None)
    return jax.shard_map(body, mesh=mesh, in_specs=in_specs, out_specs=out_specs, check_vma=False)
```

```python
import functools
import math

import jax
import jax.numpy as jnp
from jax import lax
from jax.experimental import pallas as pl
from jax.experimental.pallas import tpu as pltpu
from jax.sharding import PartitionSpec as P

HD = 128
CAP = 4
LANES = 128
GROUPS = 1
PARTS = 2
PIECES = GROUPS * PARTS
STRIDE = 6.0
NEGATIVE = -1e30
MESH = pl.DeviceIdType.MESH
F32 = jnp.float32
BF16 = jnp.bfloat16


def nt_dot(a, b):
    return lax.dot_general(a, b, (((1,), (1,)), ((), ())), preferred_element_type=F32)


def iota(shape, axis):
    return lax.broadcasted_iota(jnp.int32, shape, axis)


def kernel(
    n,
    n_dec,
    x_hbm,
    w_hbm,
    down_hbm,
    up_hbm,
    ids_hbm,
    new_hbm,
    pool_hbm,
    table_hbm,
    len_hbm,
    out_ref,
    *scratch,
):
    gathered = scratch[:PIECES]
    (
        x_ref, ids_ref, new_ref, table_ref, len_ref, w_ref, down_ref, up_ref, pages, base, shrink,
        d_send, d_recv, q_send, q_recv, keys, values, result,
        early_sem, w_sem, down_sem, up_sem, pool_sem, pool_send, pool_recv,
        up_send, low_send, across_send, side_send, side_recv, g_recv, ds_sem, dr_sem, qs_sem, qr_sem,
    ) = scratch[PIECES:]
    ada, dec = lax.axis_index("ada"), lax.axis_index("dec")
    steps, rows, width = x_ref.shape
    part = width // PARTS
    span_steps = steps // GROUPS
    block = span_steps * rows
    total = n * block
    head_cols = w_ref.shape[1]
    slots = span_steps * CAP
    span = n // 4
    o, m, c = ada // 4, (ada // 2) % 2, ada % 2
    sibling = ada + 1 - 2 * c
    opposite = ada + 2 - 4 * m
    pool_local = pool_hbm.shape[0]

    def w_copy(k):
        where = pl.ds(k * part, part)
        return pltpu.make_async_copy(w_hbm.at[where], w_ref.at[where], w_sem.at[k])

    down_copy = pltpu.make_async_copy(down_hbm, down_ref, down_sem)
    up_copy = pltpu.make_async_copy(up_hbm, up_ref, up_sem)
    own_pages = pages.at[pl.ds(dec * pool_local, pool_local)]
    pool_copy = pltpu.make_async_copy(pool_hbm, own_pages, pool_sem)

    barrier = pltpu.get_barrier_semaphore()

    def greet(peer):
        pl.semaphore_signal(barrier, inc=1, device_id={"ada": peer}, device_id_type=MESH)

    greet(opposite)
    greet(sibling)
    for side in (1, -1):

        @pl.when((o + side >= 0) & (o + side < span))
        def _():
            greet(ada + 4 * side)

    line_peers = (o >= 1).astype(jnp.int32) + (o + 1 < span).astype(jnp.int32)
    for d in range(1, n_dec):
        pl.semaphore_signal(
            barrier, inc=1, device_id={"dec": lax.rem(dec + d, n_dec)}, device_id_type=MESH
        )
    early = [
        pltpu.make_async_copy(source, target, early_sem.at[i])
        for i, (source, target) in enumerate(
            [(x_hbm, x_ref), (ids_hbm, ids_ref), (new_hbm, new_ref), (table_hbm, table_ref), (len_hbm, len_ref)]
        )
    ]
    for copy in early:
        copy.start()
    down_copy.start()
    for k in range(PARTS):
        w_copy(k).start()
    up_copy.start()
    pool_copy.start()

    early[0].wait()
    early[1].wait()
    row_of = iota((block, LANES), 0) % rows
    id_block = jnp.zeros((block, LANES), F32)
    for r in range(rows):
        id_block = jnp.where(row_of == r, ids_ref[r].astype(F32), id_block)
    gathered[0][ada, :, part : part + LANES] = id_block.astype(BF16)
    for g in range(GROUPS):
        mine = jnp.concatenate(
            [x_ref[g * span_steps + t].astype(F32) for t in range(span_steps)], axis=0
        ).astype(BF16)
        for k in range(PARTS):
            gathered[g * PARTS + k][ada, :, 0:part] = mine[:, k * part : (k + 1) * part]
    pl.semaphore_wait(barrier, line_peers + 2 + n_dec - 1)

    def relay(k, source, send_sem, peer):
        return pltpu.make_async_remote_copy(
            src_ref=gathered[k].at[source],
            dst_ref=gathered[k].at[source],
            send_sem=send_sem,
            recv_sem=g_recv.at[k, source],
            device_id={"ada": peer},
            device_id_type=MESH,
        )

    def arrived(k, source):
        relay(k, source, across_send.at[k, 0], opposite).wait_recv()

    def upward(k, line):
        return relay(k, line * 4 + m * 2 + c, up_send.at[k, line], ada + 4)

    def downward(k, line):
        return relay(k, line * 4 + m * 2 + c, low_send.at[k, line], ada - 4)

    def across(k, line):
        return relay(k, line * 4 + m * 2 + c, across_send.at[k, line], opposite)

    def sideways(k, line, column):
        source = line * 4 + column * 2 + c
        return pltpu.make_async_remote_copy(
            src_ref=gathered[k].at[source],
            dst_ref=gathered[k].at[source],
            send_sem=side_send.at[k],
            recv_sem=side_recv.at[k],
            device_id={"ada": sibling},
            device_id_type=MESH,
        )

    def all_sideways(k):
        half = gathered[k].at[pl.ds(0, n // 2)]
        return pltpu.make_async_remote_copy(
            src_ref=half,
            dst_ref=half,
            send_sem=side_send.at[k],
            recv_sem=side_recv.at[k],
            device_id={"ada": sibling},
            device_id_type=MESH,
        )

    def send_own(k):
        @pl.when(o < span - 1)
        def _():
            upward(k, o).start()

        @pl.when(o > 0)
        def _():
            downward(k, o).start()

        across(k, o).start()
        sideways(k, o, m).start()

    def line_event(k, distance):
        below, above = o - distance, o + distance

        @pl.when(below >= 0)
        def _():
            arrived(k, below * 4 + m * 2 + c)

            @pl.when(o < span - 1)
            def _():
                upward(k, below).start()

            across(k, below).start()
            sideways(k, below, m).start()

        @pl.when(above < span)
        def _():
            arrived(k, above * 4 + m * 2 + c)

            @pl.when(o > 0)
            def _():
                downward(k, above).start()

            across(k, above).start()
            sideways(k, above, m).start()

    def across_event(k, distance):
        other = 1 - m
        below, above = o - distance, o + distance

        @pl.when(below >= 0)
        def _():
            arrived(k, below * 4 + other * 2 + c)
            sideways(k, below, other).start()

        if distance:

            @pl.when(above < span)
            def _():
                arrived(k, above * 4 + other * 2 + c)
                sideways(k, above, other).start()

    def side_wave(k):
        all_sideways(k).wait_recv()

    def piece_rows(g, k):
        held = gathered[g * PARTS + k]
        return held[:, :, 0:part].reshape(total, part)

    def add_shrink(g):
        terms = [
            nt_dot(piece_rows(g, k), down_ref[:, k * part : (k + 1) * part]) for k in range(PARTS)
        ]
        shrink[g] = functools.reduce(jnp.add, terms)

    def add_base(g):
        terms = [
            jnp.dot(
                piece_rows(g, k),
                w_ref[k * part : (k + 1) * part, :],
                preferred_element_type=F32,
            )
            for k in range(PARTS)
        ]
        base[g] = functools.reduce(jnp.add, terms)

    def pool_send_copy(d):
        return pltpu.make_async_remote_copy(
            src_ref=pool_hbm,
            dst_ref=own_pages,
            send_sem=pool_send.at[d],
            recv_sem=pool_recv.at[dec],
            device_id={"dec": lax.rem(dec + d, n_dec)},
            device_id_type=MESH,
        )

    def pool_arrived(owner):
        pltpu.make_async_remote_copy(
            src_ref=pool_hbm,
            dst_ref=pages.at[pl.ds(owner * pool_local, pool_local)],
            send_sem=pool_send.at[1],
            recv_sem=pool_recv.at[owner],
            device_id={"dec": lax.rem(dec + 1, n_dec)},
            device_id_type=MESH,
        ).wait_recv()

    def slot_masks():
        id_col = jnp.concatenate(
            [gathered[0][source, :, part : part + LANES].astype(F32) for source in range(n)], axis=0
        )[:, 0:1]
        at_row, at_lane = iota((total, total), 0), iota((total, total), 1)
        id_row = jnp.sum(jnp.where(at_row == at_lane, id_col, 0.0), axis=0, keepdims=True)
        same = id_col == id_row
        row_rank = at_row // block * rows + at_row % rows
        lane_rank = at_lane // block * rows + at_lane % rows
        count_row = jnp.sum(
            jnp.where(same & (row_rank < lane_rank) & (at_row % block < rows), 1.0, 0.0),
            axis=0,
            keepdims=True,
        )
        slot, lane = iota((slots, total), 0), iota((slots, total), 1)
        pick = jnp.where(
            (slot // CAP == lane % block // rows)
            & (id_row == ada.astype(F32))
            & (count_row == (slot % CAP).astype(F32)),
            1.0,
            0.0,
        ).astype(BF16)

        def spread_mask():
            count_col = jnp.sum(
                jnp.where(same & (lane_rank < row_rank) & (at_lane % block < rows), 1.0, 0.0),
                axis=1,
                keepdims=True,
            )
            row, place = iota((total, n * slots), 0), iota((total, n * slots), 1)
            spread = jnp.where(
                (row % block // rows == place % slots // CAP)
                & (id_col == (place // slots).astype(F32))
                & (count_col == (place % CAP).astype(F32)),
                1.0,
                0.0,
            ).astype(BF16)
            return spread

        return pick, spread_mask

    entries, page = table_ref.shape[1], pages.shape[2]
    cached = rows * entries * page
    fresh_rows = steps * rows
    kv_heads = keys.shape[1] // HD
    heads = width // HD
    group = heads // kv_heads
    count = keys.shape[0]

    def key_mask(g):
        query_at, key_at = iota((heads * block, count), 0), iota((heads * block, count), 1)
        query_step, query_row = query_at % block // rows + g * span_steps, query_at % rows
        limit = jnp.zeros((heads * block, count), jnp.int32)
        for r in range(rows):
            limit = jnp.where(query_row == r, len_ref[r], limit)
        in_cache = (
            (key_at < cached)
            & (key_at // (entries * page) == query_row)
            & (key_at % (entries * page) < limit)
        )
        late = key_at - cached
        in_new = (late >= 0) & (late % rows == query_row) & (late // rows <= query_step)
        return in_cache | in_new

    def delta_of(g, chosen, target):
        columns = pl.ds(pl.multiple_of(target * head_cols, head_cols), head_cols)
        return jnp.dot(chosen, up_ref[:, columns], preferred_element_type=F32).astype(BF16)

    def d_copy(g, source, target):
        return pltpu.make_async_remote_copy(
            src_ref=d_send.at[g, target],
            dst_ref=d_recv.at[g, source],
            send_sem=ds_sem.at[g],
            recv_sem=dr_sem.at[g],
            device_id={"ada": target},
            device_id_type=MESH,
        )

    def q_copy(g, source, target):
        return pltpu.make_async_remote_copy(
            src_ref=q_send.at[g, target],
            dst_ref=q_recv.at[g, source],
            send_sem=qs_sem.at[g],
            recv_sem=qr_sem.at[g],
            device_id={"ada": target},
            device_id_type=MESH,
        )

    def others(sent, received, send_sem, recv_sem, g):
        return pltpu.make_async_remote_copy(
            src_ref=sent.at[g, pl.ds(0, n - 1)],
            dst_ref=received.at[g, pl.ds(0, n - 1)],
            send_sem=send_sem.at[g],
            recv_sem=recv_sem.at[g],
            device_id={"ada": sibling},
            device_id_type=MESH,
        )

    def all_deltas(g):
        return others(d_send, d_recv, ds_sem, dr_sem, g)

    def all_queries(g):
        return others(q_send, q_recv, qs_sem, qr_sem, g)

    order = range(1, n)
    targets = [lax.rem(ada + d, n) for d in order]

    def send_delta(g):
        chosen = jnp.dot(pick, shrink[g].astype(BF16), preferred_element_type=F32).astype(BF16)
        for i, target in enumerate(targets):
            d_send[g, target] = delta_of(g, chosen, target)
            if i > 0:
                d_copy(g, ada, targets[i - 1]).start()
        d_recv[g, ada] = delta_of(g, chosen, ada)
        d_copy(g, ada, targets[-1]).start()

    def send_query(g):
        all_deltas(g).wait_recv()
        received = d_recv[g].reshape(n * slots, head_cols)
        update = jnp.dot(spread, received, preferred_element_type=F32)
        query = base[g] + update
        q_send[g] = query.reshape(n, block, head_cols).astype(BF16)
        for target in targets:
            q_copy(g, ada, target).start()
        q_recv[g, ada] = q_send[g, ada]

    scale = 1.0 / math.sqrt(HD)
    per_source = head_cols // HD

    def attend(g, allowed):
        all_queries(g).wait_recv()
        scores = []
        for h in range(kv_heads):
            parts = []
            for j in range(group):
                head = h * group + j
                first = head % per_source * HD
                parts.append(q_recv[g, head // per_source, :, first : first + HD].astype(F32))
            query = jnp.concatenate(parts, axis=0).astype(BF16)
            scores.append(nt_dot(query, keys[:, h * HD : (h + 1) * HD]))
        scores = jnp.where(allowed, jnp.concatenate(scores, axis=0) * scale, NEGATIVE)
        top = jnp.max(scores, axis=1, keepdims=True)
        weights = jnp.where(allowed, jnp.exp(scores - top), 0.0)
        denominator = jnp.sum(weights, axis=1, keepdims=True)
        high = weights.astype(BF16)
        low = (weights - high.astype(F32)).astype(BF16)
        height = group * block
        for h in range(kv_heads):
            at, lanes = slice(h * height, (h + 1) * height), slice(h * HD, (h + 1) * HD)
            both = jnp.dot(
                jnp.concatenate([high[at], low[at]], axis=0),
                values[:, lanes],
                preferred_element_type=F32,
            )
            attended = (both[:height] + both[height:]) / denominator[at]
            for j in range(group):
                first = (h * group + j) * HD
                result[g, :, first : first + HD] = attended[j * block : (j + 1) * block]
        for t in range(span_steps):
            out_ref[g * span_steps + t] = result[g, t * rows : (t + 1) * rows, :].astype(BF16)

    events = []
    for p in range(PIECES):
        events.append((p * 1.0, 0, p, 0))
        for distance in range(1, span):
            events.append((p + STRIDE * distance, 1, p, distance))
        for distance in range(span):
            events.append((p + STRIDE * (distance + 1), 2, p, distance))
        events.append((p + STRIDE * (span + 1), 3, p, 0))
    events.sort()
    pick = spread_mask = None
    for _, kind, p, distance in events:
        if kind == 0:
            send_own(p)
            if p == min(1, PIECES - 1):
                for d in range(1, n_dec):
                    pool_send_copy(d).start()
        elif kind == 1:
            line_event(p, distance)
        elif kind == 2:
            across_event(p, distance)
        else:
            side_wave(p)
            if p == 0:
                pick, spread_mask = slot_masks()
                down_copy.wait()
                up_copy.wait()
            if p % PARTS == PARTS - 1:
                g = p // PARTS
                add_shrink(g)
                send_delta(g)
                if g == 0:
                    for k in range(PARTS):
                        w_copy(k).wait()
                if g == GROUPS - 1:
                    for i in range(g + 1):
                        add_base(i)

    for copy in early[2:]:
        copy.wait()
    spread = spread_mask()
    masks = [key_mask(g) for g in range(GROUPS)]
    pool_copy.wait()
    for d in range(1, n_dec):
        pool_arrived(lax.rem(dec + d, n_dec))
    for r in range(rows):
        for j in range(entries):
            held = pages[table_ref[r, j]]
            first = (r * entries + j) * page
            keys[first : first + page, :] = held[0]
            values[first : first + page, :] = held[1]
    fresh = [new_ref[u, r].astype(F32) for u in range(steps) for r in range(rows)]
    empty = jnp.zeros((keys.shape[0] - cached - fresh_rows, keys.shape[1]), F32)
    keys[cached:, :] = jnp.concatenate([f[0:1] for f in fresh] + [empty], axis=0).astype(BF16)
    values[cached:, :] = jnp.concatenate([f[1:2] for f in fresh] + [empty], axis=0).astype(BF16)

    for k in range(PIECES):
        all_sideways(k).wait_send()
        for line in range(span):
            across(k, line).wait_send()

            @pl.when((line <= o) & (o < span - 1))
            def _():
                upward(k, line).wait_send()

            @pl.when((line >= o) & (o > 0))
            def _():
                downward(k, line).wait_send()

    for d in range(1, n_dec):
        pool_send_copy(d).wait_send()
    for g in range(GROUPS):
        send_query(g)
    for g in range(GROUPS):
        all_deltas(g).wait_send()
    for g in range(GROUPS):
        attend(g, masks[g])

    for g in range(GROUPS):
        all_queries(g).wait_send()


def body(
    inputs,
    query_weight,
    adapter_down,
    adapter_up,
    adapter_ids,
    new_cache,
    cache_pool,
    page_table,
    lengths,
):
    n, n_dec = lax.axis_size("ada"), lax.axis_size("dec")
    steps, rows, width = inputs.shape
    held, _, rank = adapter_down.shape
    assert held == 1 and n % 4 == 0
    head_cols = query_weight.shape[1]
    block, slots, span = steps // GROUPS * rows, steps // GROUPS * CAP, n // 4
    part = width // PARTS
    pool_local, _, page, kv_width = cache_pool.shape
    count = -(-(rows * page_table.shape[1] * page + steps * rows) // 16) * 16
    dma = pltpu.SemaphoreType.DMA
    vmem, hbm = pl.BlockSpec(memory_space=pltpu.VMEM), pl.BlockSpec(memory_space=pl.ANY)
    scratch = [
        pltpu.VMEM((n, block, part + (LANES if k == 0 else 0)), BF16) for k in range(PIECES)
    ] + [
        pltpu.VMEM(inputs.shape, BF16),
        pltpu.SMEM((rows,), jnp.int32),
        pltpu.VMEM(new_cache.shape, BF16),
        pltpu.SMEM(page_table.shape, jnp.int32),
        pltpu.SMEM(lengths.shape, jnp.int32),
        pltpu.VMEM((width, head_cols), BF16),
        pltpu.VMEM((rank, width), BF16),
        pltpu.VMEM((rank, width), BF16),
        pltpu.VMEM((n_dec * pool_local, 2, page, kv_width), BF16),
        pltpu.VMEM((GROUPS, n * block, head_cols), F32),
        pltpu.VMEM((GROUPS, n * block, rank), F32),
        pltpu.VMEM((GROUPS, n, slots, head_cols), BF16),
        pltpu.VMEM((GROUPS, n, slots, head_cols), BF16),
        pltpu.VMEM((GROUPS, n, block, head_cols), BF16),
        pltpu.VMEM((GROUPS, n, block, head_cols), BF16),
        pltpu.VMEM((count, kv_width), BF16),
        pltpu.VMEM((count, kv_width), BF16),
        pltpu.VMEM((GROUPS, block, width), F32),
        dma((5,)),
        dma((PARTS,)),
        dma,
        dma,
        dma,
        dma((n_dec,)),
        dma((n_dec,)),
        dma((PIECES, span)),
        dma((PIECES, span)),
        dma((PIECES, span)),
        dma((PIECES,)),
        dma((PIECES,)),
        dma((PIECES, n)),
        dma((GROUPS,)),
        dma((GROUPS,)),
        dma((GROUPS,)),
        dma((GROUPS,)),
    ]
    return pl.pallas_call(
        functools.partial(kernel, n, n_dec),
        out_shape=pltpu.VMEM((steps, rows, width), BF16),
        in_specs=[hbm] * 9,
        out_specs=vmem,
        scratch_shapes=scratch,
        compiler_params=pltpu.CompilerParams(
            collective_id=0, has_side_effects=True, vmem_limit_bytes=60 * 1024 * 1024
        ),
    )(
        inputs,
        query_weight,
        jnp.swapaxes(adapter_down[0], 0, 1),
        adapter_up[0],
        adapter_ids[:, 0],
        new_cache,
        cache_pool,
        page_table,
        lengths,
    )


def solution(mesh):
    in_specs = (
        P(None, ("dec", "ada"), None),
        P(None, "ada"),
        P(("dec", "ada"), None, None),
        P(("dec", "ada"), None, None),
        P(("dec", "ada"), None),
        P(None, ("dec", "ada"), None, None),
        P(("dec", "ada"), None, None, None),
        P(("dec", "ada"), None),
        P(("dec", "ada")),
    )
    out_specs = P(None, ("dec", "ada"), None)
    return jax.shard_map(body, mesh=mesh, in_specs=in_specs, out_specs=out_specs, check_vma=False)
```
